32 devices in a mesh: groups: 2 (over x), req: 16 (over z, y, core).
Axes of the slice: x: 2, y: 2, z: 4, core: 2. Of those that a mesh axis runs over, the one named last changes fastest.
Arguments:
- queries: bfloat16 [64, 6, 4096], P(('groups', 'req')), parts along dimension 0, may hold values from -6 to 6
- keys: bfloat16 [64, 6, 4096], P(('groups', 'req')), parts along dimension 0, may hold values from -6 to 6
- values: bfloat16 [64, 6, 4096], P(('groups', 'req')), parts along dimension 0, may hold values from -6 to 6
- gates: bfloat16 [64, 6, 4096], P(('groups', 'req')), parts along dimension 0, may hold values from -6 to 6
- states: float32 [64, 32, 128, 128], P(('groups', 'req')), parts along dimension 0, may hold values from -12 to 12
- new_slot: int32 [64], P(('groups', 'req')), parts along dimension 0, may hold values from 0 to 31, as said below
- norm_gain: float32 [4096], replicated, may hold values from 0.1 to 1.9
Outputs:
- output: bfloat16 [64, 6, 4096], P(('groups', 'req')), parts along dimension 0
The draws below stay inside these ranges and needn't reach their ends.
There are 2 independent parts, one for each index of `groups`. The reference program is written for one: setup_inputs(seed, part) draws one part's arguments, and reference() takes and returns one part's arrays. A program takes and returns all parts, laid end to end along the dimension named above; an argument that names none is the same for every part. Nothing has to cross between parts.
Inputs may be any that keep to these rules, and one draw needn't show every extreme that they name: `new_slot`: A permutation of the slots. On one device (its 2 slots) at most 1 request change slot, and exactly 1 do on some devices; a request that changes slot never keeps it.
All inputs are finite; a program needn't handle non-finite values.
Results may differ from the reference program's by a relative error of at most 0.001.
Values sent between devices are 32-bit elements; how exact they have to be, the bound alone decides.
A program may use at most 64 MiB of HBM per device.

```python
import jax
import jax.numpy as jnp
from jax import lax

D_HEAD = 128
HEADS = 32
SLOTS_DEV = 2
BEFORE = 3
STEPS = 6
MOVE_DEV = 1
REQUESTS = 32
WIDTH = 4096


def draw_states(key, part):
    key_scale, key_base = jax.random.split(key, 2)
    shape = (REQUESTS, HEADS, D_HEAD, D_HEAD)
    scales = jnp.exp(jax.random.uniform(key_scale, (REQUESTS, HEADS, 1, 1), jnp.float32, jnp.log(0.3), jnp.log(3.0)))
    return jnp.clip(jax.random.normal(key_base, shape, jnp.float32), -4.0, 4.0) * scales


def draw_new_slot(key, part):
    device_count = REQUESTS // SLOTS_DEV
    key_count, key_first, key_rank, key_order = jax.random.split(key, 4)
    counts = jax.random.randint(key_count, (device_count,), 0, MOVE_DEV + 1)
    first = jax.random.randint(key_first, (), 0, device_count)
    marks = jnp.arange(device_count)
    forced = (marks == first) | (marks == (first + 1) % device_count)
    counts = jnp.where(forced, MOVE_DEV, counts)
    ranks = jax.vmap(lambda sub: jax.random.permutation(sub, SLOTS_DEV))(jax.random.split(key_rank, device_count))
    moving = (ranks < counts[:, None]).reshape(-1)
    order_key = jax.random.permutation(key_order, REQUESTS)
    score = jnp.where(moving, order_key, REQUESTS + order_key)
    order = jnp.argsort(score, stable=True).astype(jnp.int32)
    moving_total = jnp.sum(moving.astype(jnp.int32))
    positions = jnp.arange(REQUESTS).astype(jnp.int32)
    following = order[(positions + 1) % moving_total]
    target = jnp.where(positions < moving_total, following, order)
    return jnp.zeros((REQUESTS,), jnp.int32).at[order].set(target.astype(jnp.int32))


def shard_levels(key, extent, cuts, low, high):
    factor_of = 1.0
    for position, shards_of in cuts:
        heights = jax.random.uniform(jax.random.fold_in(jax.random.fold_in(key, 6), position), (shards_of,), jnp.float32, low / len(cuts), high / len(cuts))
        factor_of = factor_of * jnp.repeat(jnp.exp(heights), extent[position] // shards_of).reshape((-1,) + (1,) * (len(extent) - 1 - position))
    return factor_of


def noise(rng, dims, scale, reach, cuts=(), dtype=jnp.bfloat16):
    factor_of = shard_levels(rng, dims, cuts, -0.22, 0.18) if cuts else 1.0
    result = jax.random.normal(rng, dims, jnp.float32) * scale * factor_of
    return jnp.minimum(jnp.maximum(result, -reach), reach).astype(dtype)


def setup_inputs(seed: int = 0, part: int = 0) -> dict:
    streams_of = jax.random.split(jax.random.key(seed), 8)
    part_splits = jax.random.split(jax.random.fold_in(streams_of[7], part), 8)
    return {
        "queries": noise(part_splits[0], (REQUESTS, STEPS, WIDTH), 1.0, 6.0, ((0, 16),)),
        "keys": noise(part_splits[1], (REQUESTS, STEPS, WIDTH), 1.0, 6.0, ((0, 16),)),
        "values": noise(part_splits[2], (REQUESTS, STEPS, WIDTH), 1.0, 6.0, ((0, 16),)),
        "gates": noise(part_splits[3], (REQUESTS, STEPS, WIDTH), 1.0, 6.0, ((0, 16),)),
        "states": draw_states(jax.random.fold_in(jax.random.fold_in(streams_of[7], part), 71), part),
        "new_slot": draw_new_slot(jax.random.fold_in(jax.random.fold_in(streams_of[7], part), 71), part),
        "norm_gain": jnp.clip(1.0 + 0.18 * jax.random.normal(streams_of[6], (WIDTH,), jnp.float32), 0.1, 1.9),
    }


def head_decay():
    order = jnp.arange(HEADS).astype(jnp.float32)
    slope = 2.0 ** (-8.0 * (order + 1.0) / (2.0 * HEADS))
    return jnp.exp(-slope)

def advance(current, query_row, key_row, value_row, gate_row, norm_gain):
    count = current.shape[0]
    query_act = jax.nn.silu(query_row.astype(jnp.float32)).reshape(count, HEADS, D_HEAD)
    key_act = jax.nn.silu(key_row.astype(jnp.float32)).reshape(count, HEADS, D_HEAD)
    value_act = jax.nn.silu(value_row.astype(jnp.float32)).reshape(count, HEADS, D_HEAD)
    current = head_decay()[None, :, None, None] * current + key_act[:, :, :, None] * value_act[:, :, None, :]
    mixed = jnp.einsum('nhi,nhij->nhj', query_act, current, precision=lax.Precision.HIGHEST)
    mixed = mixed.reshape(count, HEADS * D_HEAD)
    energy = lax.optimization_barrier(jnp.mean(mixed * mixed, axis=-1, keepdims=True))
    output = mixed * lax.rsqrt(energy + 1e-06) * norm_gain[None, :] * jax.nn.sigmoid(gate_row.astype(jnp.float32))
    return (current, output.astype(jnp.bfloat16))

def reference(queries, keys, values, gates, states, new_slot, norm_gain):

    def opening(request):
        current = states[request][None]
        row_list = []
        for moment in range(BEFORE):
            current, row = advance(current, queries[request, moment][None], keys[request, moment][None], values[request, moment][None], gates[request, moment][None], norm_gain)
            row_list.append(row[0])
        return (current[0], jnp.stack(row_list))
    slot_ids = jnp.arange(REQUESTS).astype(jnp.int32)
    mid_states, early_rows = lax.map(opening, slot_ids)
    inverse = jnp.zeros((REQUESTS,), jnp.int32).at[new_slot].set(slot_ids)

    def later(slot):
        anchor = inverse[slot]
        current = mid_states[anchor][None]
        row_list = []
        for moment in range(BEFORE, STEPS):
            current, row = advance(current, queries[slot, moment][None], keys[slot, moment][None], values[slot, moment][None], gates[slot, moment][None], norm_gain)
            row_list.append(row[0])
        return jnp.concatenate([early_rows[slot], jnp.stack(row_list)], axis=0)
    return lax.map(later, slot_ids)
```

```python
import functools
import math

import jax
import jax.numpy as jnp
from jax import lax
from jax.experimental import pallas as pl
from jax.experimental.pallas import tpu as pltpu
from jax.sharding import PartitionSpec as P

D_HEAD = 128
BEFORE = 3
STEPS = 6
MODEL_HEADS = 64
GROUP = STEPS - BEFORE
LEAD = 8

MESH = pl.DeviceIdType.MESH


def silu(x):
    return x / (1.0 + jnp.exp(-x))


def split(x):
    high = x.astype(jnp.bfloat16).astype(jnp.float32)
    return high, x - high


def rows_of(src, dst):
    for t in range(STEPS):
        both = src[t].astype(jnp.float32)
        for s in range(both.shape[0]):
            dst[s, t : t + 1, :] = both[s : s + 1]


def head_slope(heads):
    return jnp.exp((heads + 1.0) * (-8.0 / MODEL_HEADS * math.log(2.0)))


def kernel(
    count,
    hubs,
    slot_hbm,
    q_hbm,
    k_hbm,
    v_hbm,
    g_hbm,
    gain_hbm,
    s_hbm,
    out_ref,
    slot_ref,
    q_v,
    k_v,
    v_v,
    g_v,
    gain_v,
    s_v,
    s_pair,
    a_v,
    b_v,
    c_v,
    w_v,
    base_v,
    scale_v,
    row_v,
    early_k,
    early_v,
    piece,
    hub_in,
    hub_out,
    q_in,
    r_out,
    hub_r,
    hub_f,
    final,
    load_sem,
    state_sem,
    send_a,
    recv_a,
    send_b,
    recv_b,
    send_c,
    recv_c,
    send_d,
    recv_d,
):
    slots, heads = s_hbm.shape[0], s_hbm.shape[1]
    width = heads * D_HEAD
    per_hub = heads // hubs
    rows = GROUP * per_hub
    room = piece.shape[1]
    first = count // 2 - hubs
    me = lax.axis_index("req")
    is_hub = (me >= first) & (me < first + 2 * hubs) & (lax.rem(me, 2) == 1)
    hub_rank = jnp.clip(me - first, 0, 2 * hubs - 1) // 2

    def hub_at(j):
        return first + 2 * j + 1

    loads = [
        pltpu.make_async_copy(src, dst, load_sem.at[k])
        for k, (src, dst) in enumerate(
            (
                (slot_hbm, slot_ref),
                (q_hbm, q_v),
                (k_hbm, k_v),
                (v_hbm, v_v),
                (g_hbm, g_v),
                (gain_hbm, gain_v),
            )
        )
    ]
    state_loads = [
        pltpu.make_async_copy(s_hbm.at[s], s_v.at[s], state_sem.at[s]) for s in range(slots)
    ]
    loads[0].start()
    loads[1].start()

    barrier = pltpu.get_barrier_semaphore()

    def other(k):
        return lax.rem(me + k, count)

    @pl.when(is_hub)
    def _():
        def greet(k, carry):
            pl.semaphore_signal(barrier, inc=1, device_id={"req": other(k)}, device_id_type=MESH)
            return carry

        lax.fori_loop(1, count, greet, 0, unroll=5 if (count - 1) % 5 == 0 else 1)

    for copy in loads[2:4] + state_loads + loads[4:]:
        copy.start()

    loads[0].wait()
    moving = jnp.int32(0)
    for s in range(slots):
        moving = jnp.where(slot_ref[s] != me * slots + s, jnp.int32(s), moving)
    wanted = slot_ref[moving] // slots
    wanted_row = jnp.full((1, D_HEAD), wanted, jnp.int32).astype(jnp.float32)

    loads[1].wait()
    rows_of(q_v, a_v)
    for s in range(slots):
        a_v[s, 0:STEPS, :] = silu(a_v[s, 0:STEPS, :])
        a_v[s, STEPS:, :] = jnp.zeros((8 - STEPS, width), jnp.float32)
    for h in range(heads):
        j, hh = divmod(h, per_hub)
        piece[j, GROUP * hh : GROUP * hh + GROUP, :] = a_v[
            moving, BEFORE:STEPS, h * D_HEAD : (h + 1) * D_HEAD
        ]
    for j in range(hubs):
        piece[j, rows : rows + 1, :] = wanted_row

    @pl.when(is_hub)
    def _():
        hub_in[me] = piece[hub_rank]

    @pl.when(is_hub)
    def _():
        if hubs > 1:
            pl.semaphore_wait(barrier, hubs - 1)

    @pl.when(jnp.logical_not(is_hub))
    def _():
        pl.semaphore_wait(barrier, hubs)

    def remote(src, dst, send, recv, target):
        return pltpu.make_async_remote_copy(
            src_ref=src,
            dst_ref=dst,
            send_sem=send,
            recv_sem=recv,
            device_id={"req": target},
            device_id_type=MESH,
        )

    def arrive(dst, recv):
        pltpu.make_async_copy(dst, dst, recv).wait()

    def each_hub(act):
        for j in range(hubs):

            @pl.when(hub_at(j) != me)
            def _():
                act(j)

    def to_hub_first(j):
        return remote(
            piece.at[j, 0 : rows + 1],
            hub_in.at[me, 0 : rows + 1],
            send_a.at[j],
            recv_a.at[me],
            hub_at(j),
        )

    def to_hub_back(j):
        return remote(
            r_out.at[j, 0:rows], hub_r.at[me, 0:rows], send_c.at[j], recv_c.at[me], hub_at(j)
        )

    def from_hub_first(i):
        return remote(
            hub_out.at[i, 0:rows], q_in.at[hub_rank, 0:rows], send_b.at[i], recv_b.at[hub_rank], i
        )

    final_at = pl.multiple_of(LEAD + room * hub_rank, 8)

    def from_hub_back(i):
        return remote(
            hub_f.at[i, 0:rows],
            final.at[pl.ds(final_at, rows)],
            send_d.at[i],
            recv_d.at[hub_rank],
            i,
        )

    far = jnp.where(me >= count // 2, 0, max(1, hubs // 2))
    for jj in range(hubs):
        far_j = lax.rem(far + jj, hubs)

        @pl.when(hub_at(far_j) != me)
        def _():
            to_hub_first(far_j).start()


    loads[2].wait()
    loads[3].wait()
    rows_of(k_v, b_v)
    rows_of(v_v, c_v)
    for s in range(slots):
        b_v[s, 0:STEPS, :] = silu(b_v[s, 0:STEPS, :])
        c_v[s, 0:STEPS, :] = silu(c_v[s, 0:STEPS, :])
        b_v[s, STEPS:, :] = jnp.zeros((8 - STEPS, width), jnp.float32)
        c_v[s, STEPS:, :] = jnp.zeros((8 - STEPS, width), jnp.float32)

    for copy in state_loads:
        copy.wait()

    def halve(h, carry):
        for s in range(slots):
            high, low = split(s_v[s, h])
            s_pair[s, h, 0:D_HEAD, :] = high.astype(jnp.bfloat16)
            s_pair[s, h, D_HEAD:, :] = low.astype(jnp.bfloat16)
        return carry

    lax.fori_loop(0, heads, halve, 0, unroll=2)

    planes = count // hubs
    near = planes // 2 - 1
    order = sorted(range(planes), key=lambda p: (-abs(p - near), -p))
    own_plane = me // hubs
    own_lane = lax.rem(me, hubs)

    def far_first(k):
        place = k // hubs
        plane = order[-1]
        for p in range(planes - 1):
            plane = jnp.where(place == p, order[p], plane)
        plane = jnp.where(own_plane == near, plane, planes - 1 - plane)
        lane = own_lane + lax.rem(k, hubs) + jnp.where(plane == own_plane, 1, 0)
        return plane * hubs + lax.rem(lane, hubs)

    def in_turn(k):
        return k + jnp.where(k >= me, 1, 0)

    hub_unroll = 5 if (count - 1) % 5 == 0 else 1

    @pl.when(is_hub)
    def _():
        for k in range(1, count):
            e = other(k)
            arrive(hub_in.at[e, 0 : rows + 1], recv_a.at[e])

        def choose(i):
            want = hub_in[i, rows : rows + 1, :]
            chosen = hub_in[0, 0:rows]
            for e in range(1, count):
                chosen = jnp.where(want == float(e), hub_in[e, 0:rows], chosen)
            return chosen

        def hand(k, carry):
            i = far_first(k)
            hub_out[i, 0:rows] = choose(i)
            from_hub_first(i).start()
            return carry

        lax.fori_loop(0, count - 1, hand, 0, unroll=hub_unroll)
        q_in[hub_rank, 0:rows] = choose(me)

    piece_row = lax.broadcasted_iota(jnp.int32, (room, D_HEAD), 0)
    piece_head = jnp.zeros((room, D_HEAD), jnp.int32)
    for hh in range(1, per_hub):
        piece_head = jnp.where(piece_row >= GROUP * hh, hh, piece_head)
    piece_step = (piece_row - GROUP * piece_head).astype(jnp.float32)
    for h in range(heads):
        j, hh = divmod(h, per_hub)
        cols = slice(h * D_HEAD, (h + 1) * D_HEAD)
        for s in range(BEFORE):
            early_k[s, j, GROUP * hh : GROUP * (hh + 1), :] = jnp.broadcast_to(
                b_v[moving, s : s + 1, cols], (GROUP, D_HEAD)
            )
            early_v[s, j, GROUP * hh : GROUP * (hh + 1), :] = jnp.broadcast_to(
                c_v[moving, s : s + 1, cols], (GROUP, D_HEAD)
            )

    step = lax.broadcasted_iota(jnp.int32, (8, D_HEAD), 0)
    step_f = step.astype(jnp.float32)

    def own(h, carry):
        cols = pl.ds(pl.multiple_of(h * D_HEAD, D_HEAD), D_HEAD)
        slope = head_slope(jnp.full((8, D_HEAD), h, jnp.int32).astype(jnp.float32))
        decay_state = jnp.exp(-slope * (step_f + 1.0))
        for s in range(slots):
            a, b, c = a_v[s, :, cols], b_v[s, :, cols], c_v[s, :, cols]
            high, low = split(a)
            left = jnp.concatenate([high, low], axis=0)
            left = jnp.concatenate([left, left], axis=1).astype(jnp.bfloat16)
            both = jnp.dot(left, s_pair[s, h], preferred_element_type=jnp.float32)
            base = decay_state * (both[:8] + both[8:])
            within = jnp.zeros((8, D_HEAD), jnp.float32)
            for back in range(STEPS):
                b_back = pltpu.roll(b, back, 0) if back else b
                c_back = pltpu.roll(c, back, 0) if back else c
                mix = jnp.sum(a * b_back, axis=1, keepdims=True)
                term = mix * c_back * jnp.exp(-slope * float(back))
                late = (step >= BEFORE) & (step < STEPS)
                if back < BEFORE:
                    keep = ((step < BEFORE) & (step >= back)) | (late & (step >= BEFORE + back))
                    within = within + jnp.where(keep, term, 0.0)
                if back:
                    cross = late & (step >= back) & (step < BEFORE + back)
                    base = base + jnp.where(cross, term, 0.0)
            base_v[s, :, cols] = base
            w_v[s, :, cols] = within
        return carry

    lax.fori_loop(0, heads, own, 0, unroll=2)

    def answer(j):
        q = q_in[j]
        high, low = split(q)
        left = jnp.concatenate([high, low], axis=0)
        left = jnp.concatenate([left, left], axis=1).astype(jnp.bfloat16)
        slope = head_slope((piece_head + j * per_hub).astype(jnp.float32))
        total = jnp.zeros((room, D_HEAD), jnp.float32)
        for hh in range(per_hub):
            both = jnp.dot(
                left, s_pair[moving, j * per_hub + hh], preferred_element_type=jnp.float32
            )
            total = jnp.where(piece_head == hh, both[:room] + both[room:], total)
        total = total * jnp.exp(-slope * (piece_step + (BEFORE + 1.0)))
        for s in range(BEFORE):
            mix = jnp.sum(q * early_k[s, j], axis=1, keepdims=True)
            total = total + mix * early_v[s, j] * jnp.exp(
                -slope * (piece_step + float(BEFORE - s))
            )
        r_out[j] = total

    split_at = max(1, hubs // 2)
    turn = jnp.where(me >= count // 2, split_at, 0)
    share = max(1, hubs // 4)
    for group in [range(k, min(k + share, hubs)) for k in range(0, hubs, share)]:
        order = [lax.rem(turn + jj, hubs) for jj in group]

        def others(act):
            for j in order:

                @pl.when(hub_at(j) != me)
                def _():
                    act(j)

        others(lambda j: arrive(q_in.at[j, 0:rows], recv_b.at[j]))
        for j in order:
            answer(j)
        others(lambda j: to_hub_back(j).start())

    @pl.when(is_hub)
    def _():
        hub_r[me] = r_out[hub_rank]

    loads[4].wait()
    loads[5].wait()
    rows_of(g_v, scale_v)
    for s in range(slots):
        gate = scale_v[s, 0:STEPS, :]
        scale_v[s, 0:STEPS, :] = gain_v[...] / (1.0 + jnp.exp(-gate))
        scale_v[s, STEPS:, :] = jnp.zeros((8 - STEPS, width), jnp.float32)
    for s in range(slots):
        mixed = base_v[s] + w_v[s]
        energy = jnp.sum(mixed * mixed, axis=1, keepdims=True) * (1.0 / width)
        row = mixed * lax.rsqrt(energy + 1e-06) * scale_v[s]
        for t in range(STEPS):
            row_v[t, s : s + 1, :] = row[t : t + 1]
    for t in range(BEFORE):
        out_ref[t] = row_v[t].astype(out_ref.dtype)

    @pl.when(is_hub)
    def _():
        for k in range(1, count):
            e = other(k)
            arrive(hub_r.at[e, 0:rows], recv_c.at[e])

        def choose(i):
            place = jnp.full((1, D_HEAD), i, jnp.int32).astype(jnp.float32)
            chosen = hub_r[0, 0:rows]
            for e in range(1, count):
                chosen = jnp.where(hub_in[e, rows : rows + 1, :] == place, hub_r[e, 0:rows], chosen)
            return chosen

        def back(k, carry):
            i = in_turn(k)
            hub_f[i, 0:rows] = choose(i)
            from_hub_back(i).start()
            return carry

        lax.fori_loop(0, count - 1, back, 0, unroll=hub_unroll)
        final[pl.ds(final_at, rows), :] = choose(me)

    each_hub(lambda j: arrive(final.at[pl.ds(LEAD + room * j, rows)], recv_d.at[j]))

    square = jnp.zeros((8, D_HEAD), jnp.float32)
    mixed = []
    for h in range(heads):
        top = LEAD + room * (h // per_hub) + GROUP * (h % per_hub) - BEFORE
        got = final[top : top + 8, :] + w_v[moving, :, h * D_HEAD : (h + 1) * D_HEAD]
        square = square + got * got
        mixed.append(got)
    energy = jnp.sum(square, axis=1, keepdims=True) * (1.0 / width)
    inverse = lax.rsqrt(energy + 1e-06)
    moved = lax.broadcasted_iota(jnp.int32, (slots, D_HEAD), 0) == moving
    for h in range(heads):
        cols = slice(h * D_HEAD, (h + 1) * D_HEAD)
        row = mixed[h] * inverse * scale_v[moving, :, cols]
        for t in range(BEFORE, STEPS):
            value = jnp.where(
                moved, jnp.broadcast_to(row[t : t + 1], (slots, D_HEAD)), row_v[t, :, cols]
            )
            out_ref[t, :, cols] = value.astype(out_ref.dtype)

    each_hub(lambda j: to_hub_first(j).wait_send())
    each_hub(lambda j: to_hub_back(j).wait_send())

    @pl.when(is_hub)
    def _():
        def drain(k, carry):
            from_hub_first(other(k)).wait_send()
            from_hub_back(other(k)).wait_send()
            return carry

        lax.fori_loop(1, count, drain, 0)


def on_device(queries, keys, values, gates, states, new_slot, norm_gain):
    queries, keys, values, gates = (x.transpose(1, 0, 2) for x in (queries, keys, values, gates))
    steps, slots, width = queries.shape
    heads = states.shape[1]
    count = lax.axis_size("req")
    hubs = max(1, min(count // 4, heads // 2))
    room = -(-(GROUP * (heads // hubs) + 1) // 8) * 8
    f32, bf16 = jnp.float32, jnp.bfloat16
    hbm = pl.BlockSpec(memory_space=pl.ANY)
    dma = pltpu.SemaphoreType.DMA
    slab = pltpu.VMEM((slots, 8, width), f32)
    return pl.pallas_call(
        functools.partial(kernel, count, hubs),
        out_shape=pltpu.VMEM(queries.shape, queries.dtype),
        in_specs=[hbm] * 7,
        out_specs=pl.BlockSpec(memory_space=pltpu.VMEM),
        scratch_shapes=[
            pltpu.SMEM(new_slot.shape, new_slot.dtype),
            pltpu.VMEM(queries.shape, bf16),
            pltpu.VMEM(queries.shape, bf16),
            pltpu.VMEM(queries.shape, bf16),
            pltpu.VMEM(queries.shape, bf16),
            pltpu.VMEM((1, width), f32),
            pltpu.VMEM(states.shape, f32),
            pltpu.VMEM((slots, heads, 2 * D_HEAD, D_HEAD), bf16),
            slab,
            slab,
            slab,
            slab,
            slab,
            slab,
            pltpu.VMEM((steps, slots, width), f32),
            pltpu.VMEM((BEFORE, hubs, room, D_HEAD), f32),
            pltpu.VMEM((BEFORE, hubs, room, D_HEAD), f32),
            pltpu.VMEM((hubs, room, D_HEAD), f32),
            pltpu.VMEM((count, room, D_HEAD), f32),
            pltpu.VMEM((count, room, D_HEAD), f32),
            pltpu.VMEM((hubs, room, D_HEAD), f32),
            pltpu.VMEM((hubs, room, D_HEAD), f32),
            pltpu.VMEM((count, room, D_HEAD), f32),
            pltpu.VMEM((count, room, D_HEAD), f32),
            pltpu.VMEM((LEAD + room * hubs + 8, D_HEAD), f32),
            dma((6,)),
            dma((slots,)),
            dma((hubs,)),
            dma((count,)),
            dma((count,)),
            dma((hubs,)),
            dma((hubs,)),
            dma((count,)),
            dma((count,)),
            dma((hubs,)),
        ],
        compiler_params=pltpu.CompilerParams(collective_id=0, has_side_effects=True),
    )(new_slot, queries, keys, values, gates, norm_gain.reshape(1, width), states).transpose(
        1, 0, 2
    )


def solution(mesh):
    in_specs = (
        P(("groups", "req"), None, None),
        P(("groups", "req"), None, None),
        P(("groups", "req"), None, None),
        P(("groups", "req"), None, None),
        P(("groups", "req"), None, None, None),
        P(("groups", "req")),
        P(),
    )
    out_specs = P(("groups", "req"), None, None)
    return jax.shard_map(
        on_device, mesh=mesh, in_specs=in_specs, out_specs=out_specs, check_vma=False
    )
```

```python
import functools
import math

import jax
import jax.numpy as jnp
from jax import lax
from jax.experimental import pallas as pl
from jax.experimental.pallas import tpu as pltpu
from jax.sharding import PartitionSpec as P

D_HEAD = 128
BEFORE = 3
STEPS = 6
MODEL_HEADS = 64
GROUP = STEPS - BEFORE
LEAD = 8

MESH = pl.DeviceIdType.MESH


def silu(x):
    return x / (1.0 + jnp.exp(-x))


def split(x):
    high = x.astype(jnp.bfloat16).astype(jnp.float32)
    return high, x - high


def rows_of(src, dst):
    for t in range(STEPS):
        both = src[t].astype(jnp.float32)
        for s in range(both.shape[0]):
            dst[s, t : t + 1, :] = both[s : s + 1]


def head_slope(heads):
    return jnp.exp((heads + 1.0) * (-8.0 / MODEL_HEADS * math.log(2.0)))


def kernel(
    count,
    hubs,
    slot_hbm,
    q_hbm,
    k_hbm,
    v_hbm,
    g_hbm,
    gain_hbm,
    s_hbm,
    out_ref,
    slot_ref,
    q_v,
    k_v,
    v_v,
    g_v,
    gain_v,
    s_v,
    s_pair,
    a_v,
    b_v,
    c_v,
    w_v,
    base_v,
    scale_v,
    row_v,
    early_k,
    early_v,
    fade,
    piece,
    hub_in,
    hub_out,
    q_in,
    r_out,
    hub_r,
    hub_f,
    final,
    load_sem,
    state_sem,
    send_a,
    recv_a,
    send_b,
    recv_b,
    send_c,
    recv_c,
    send_d,
    recv_d,
):
    slots, heads = s_hbm.shape[0], s_hbm.shape[1]
    width = heads * D_HEAD
    per_hub = heads // hubs
    rows = GROUP * per_hub
    room = piece.shape[1]
    first = count // 2 - hubs
    me = lax.axis_index("req")
    is_hub = (me >= first) & (me < first + 2 * hubs) & (lax.rem(me, 2) == 1)
    hub_rank = jnp.clip(me - first, 0, 2 * hubs - 1) // 2

    def hub_at(j):
        return first + 2 * j + 1

    loads = [
        pltpu.make_async_copy(src, dst, load_sem.at[k])
        for k, (src, dst) in enumerate(
            (
                (slot_hbm, slot_ref),
                (q_hbm.at[BEFORE:], q_v.at[BEFORE:]),
                (q_hbm.at[:BEFORE], q_v.at[:BEFORE]),
                (k_hbm, k_v),
                (v_hbm, v_v),
                (g_hbm, g_v),
                (gain_hbm, gain_v),
            )
        )
    ]
    state_loads = [
        pltpu.make_async_copy(s_hbm.at[s], s_v.at[s], state_sem.at[s]) for s in range(slots)
    ]
    loads[0].start()
    loads[1].start()

    barrier = pltpu.get_barrier_semaphore()

    def other(k):
        return lax.rem(me + k, count)

    @pl.when(is_hub)
    def _():
        def greet(k, carry):
            pl.semaphore_signal(barrier, inc=1, device_id={"req": other(k)}, device_id_type=MESH)
            return carry

        lax.fori_loop(1, count, greet, 0, unroll=5 if (count - 1) % 5 == 0 else 1)

    for copy in loads[2:5] + state_loads + loads[5:]:
        copy.start()

    loads[0].wait()
    moving = jnp.int32(0)
    for s in range(slots):
        moving = jnp.where(slot_ref[s] != me * slots + s, jnp.int32(s), moving)
    wanted = slot_ref[moving] // slots
    wanted_row = jnp.full((1, D_HEAD), wanted, jnp.int32).astype(jnp.float32)

    loads[1].wait()
    span = per_hub * D_HEAD

    def pack(j, carry):
        cols = pl.ds(pl.multiple_of(j * span, D_HEAD), span)
        for t in range(GROUP):
            both = q_v[BEFORE + t, :, cols].astype(jnp.float32)
            raw = both[0:1]
            for s in range(1, slots):
                raw = jnp.where(moving == s, both[s : s + 1], raw)
            for hh in range(per_hub):
                row = GROUP * hh + t
                piece[j, row : row + 1, :] = raw[:, hh * D_HEAD : (hh + 1) * D_HEAD]
        piece[j, 0:rows, :] = silu(piece[j, 0:rows, :])
        piece[j, rows : rows + 1, :] = wanted_row
        return carry

    lax.fori_loop(0, hubs, pack, 0)

    @pl.when(is_hub)
    def _():
        hub_in[me] = piece[hub_rank]

    @pl.when(is_hub)
    def _():
        if hubs > 1:
            pl.semaphore_wait(barrier, hubs - 1)

    @pl.when(jnp.logical_not(is_hub))
    def _():
        pl.semaphore_wait(barrier, hubs)

    def remote(src, dst, send, recv, target):
        return pltpu.make_async_remote_copy(
            src_ref=src,
            dst_ref=dst,
            send_sem=send,
            recv_sem=recv,
            device_id={"req": target},
            device_id_type=MESH,
        )

    def arrive(dst, recv):
        pltpu.make_async_copy(dst, dst, recv).wait()

    def each_hub(act):
        for j in range(hubs):

            @pl.when(hub_at(j) != me)
            def _():
                act(j)

    def to_hub_first(j):
        return remote(
            piece.at[j, 0 : rows + 1],
            hub_in.at[me, 0 : rows + 1],
            send_a.at[j],
            recv_a.at[me],
            hub_at(j),
        )

    def to_hub_back(j):
        return remote(
            r_out.at[j, 0:rows], hub_r.at[me, 0:rows], send_c.at[j], recv_c.at[me], hub_at(j)
        )

    def from_hub_first(i):
        return remote(
            hub_out.at[i, 0:rows], q_in.at[hub_rank, 0:rows], send_b.at[i], recv_b.at[hub_rank], i
        )

    final_at = pl.multiple_of(LEAD + room * hub_rank, 8)

    def from_hub_back(i):
        return remote(
            hub_f.at[i, 0:rows],
            final.at[pl.ds(final_at, rows)],
            send_d.at[i],
            recv_d.at[hub_rank],
            i,
        )

    far = jnp.where(me >= count // 2, 0, max(1, hubs // 2))
    for jj in range(hubs):
        far_j = lax.rem(far + jj, hubs)

        @pl.when(hub_at(far_j) != me)
        def _():
            to_hub_first(far_j).start()

    loads[2].wait()
    rows_of(q_v, a_v)
    for s in range(slots):
        a_v[s, 0:STEPS, :] = silu(a_v[s, 0:STEPS, :])
        a_v[s, STEPS:, :] = jnp.zeros((8 - STEPS, width), jnp.float32)
    loads[3].wait()
    loads[4].wait()
    rows_of(k_v, b_v)
    rows_of(v_v, c_v)
    for s in range(slots):
        b_v[s, 0:STEPS, :] = silu(b_v[s, 0:STEPS, :])
        c_v[s, 0:STEPS, :] = silu(c_v[s, 0:STEPS, :])
        b_v[s, STEPS:, :] = jnp.zeros((8 - STEPS, width), jnp.float32)
        c_v[s, STEPS:, :] = jnp.zeros((8 - STEPS, width), jnp.float32)

    for copy in state_loads:
        copy.wait()

    def halve(h, carry):
        for s in range(slots):
            for side in range(2):
                cols = slice(side * D_HEAD, (side + 1) * D_HEAD)
                high, low = split(s_v[s, 2 * h + side])
                s_pair[s, h, 0:D_HEAD, cols] = high.astype(jnp.bfloat16)
                s_pair[s, h, D_HEAD:, cols] = low.astype(jnp.bfloat16)
        return carry

    lax.fori_loop(0, heads // 2, halve, 0)

    planes = count // hubs
    near = planes // 2 - 1
    order = sorted(range(planes), key=lambda p: (-abs(p - near), -p))
    own_plane = me // hubs
    own_lane = lax.rem(me, hubs)

    def far_first(k):
        place = k // hubs
        plane = order[-1]
        for p in range(planes - 1):
            plane = jnp.where(place == p, order[p], plane)
        plane = jnp.where(own_plane == near, plane, planes - 1 - plane)
        lane = own_lane + lax.rem(k, hubs) + jnp.where(plane == own_plane, 1, 0)
        return plane * hubs + lax.rem(lane, hubs)

    def in_turn(k):
        return k + jnp.where(k >= me, 1, 0)

    hub_unroll = 5 if (count - 1) % 5 == 0 else 1

    @pl.when(is_hub)
    def _():
        def gather(k, carry):
            arrive(hub_in.at[other(k), 0 : rows + 1], recv_a.at[other(k)])
            return carry

        lax.fori_loop(1, count, gather, 0)

        def choose(i):
            want = hub_in[i, rows : rows + 1, :]
            chosen = hub_in[0, 0:rows]
            for e in range(1, count):
                chosen = jnp.where(want == float(e), hub_in[e, 0:rows], chosen)
            return chosen

        def hand(k, carry):
            i = far_first(k)
            hub_out[i, 0:rows] = choose(i)
            from_hub_first(i).start()
            return carry

        lax.fori_loop(0, count - 1, hand, 0, unroll=hub_unroll)
        q_in[hub_rank, 0:rows] = choose(me)

    piece_row = lax.broadcasted_iota(jnp.int32, (rows, D_HEAD), 0)
    piece_head = jnp.zeros((rows, D_HEAD), jnp.int32)
    for hh in range(1, per_hub):
        piece_head = jnp.where(piece_row >= GROUP * hh, hh, piece_head)
    piece_step = (piece_row - GROUP * piece_head).astype(jnp.float32)
    def fading(j, carry):
        slope = head_slope((piece_head + j * per_hub).astype(jnp.float32))
        fade[j, 0] = jnp.exp(-slope * (piece_step + (BEFORE + 1.0)))
        for s in range(BEFORE):
            fade[j, 1 + s] = jnp.exp(-slope * (piece_step + float(BEFORE - s)))
        return carry

    lax.fori_loop(0, hubs, fading, 0)
    for h in range(heads):
        j, hh = divmod(h, per_hub)
        cols = slice(h * D_HEAD, (h + 1) * D_HEAD)
        for s in range(BEFORE):
            early_k[s, j, GROUP * hh : GROUP * (hh + 1), :] = jnp.broadcast_to(
                b_v[moving, s : s + 1, cols], (GROUP, D_HEAD)
            )
            early_v[s, j, GROUP * hh : GROUP * (hh + 1), :] = jnp.broadcast_to(
                c_v[moving, s : s + 1, cols], (GROUP, D_HEAD)
            )

    step = lax.broadcasted_iota(jnp.int32, (8, D_HEAD), 0)
    step_f = step.astype(jnp.float32)

    def own(pair, carry):
        for s in range(slots):
            wide = pl.ds(pl.multiple_of(pair * 2 * D_HEAD, D_HEAD), 2 * D_HEAD)
            a_high, a_low = split(a_v[s, :, wide])
            for side in range(2):
                h = 2 * pair + side
                here = slice(side * D_HEAD, (side + 1) * D_HEAD)
                cols = pl.ds(pl.multiple_of(h * D_HEAD, D_HEAD), D_HEAD)
                slope = head_slope(jnp.full((8, D_HEAD), h, jnp.int32).astype(jnp.float32))
                decay_state = jnp.exp(-slope * (step_f + 1.0))
                a, b, c = a_v[s, :, cols], b_v[s, :, cols], c_v[s, :, cols]
                left = jnp.concatenate([a_high[:, here], a_low[:, here]], axis=0)
                left = jnp.concatenate([left, left], axis=1).astype(jnp.bfloat16)
                both = jnp.dot(
                    left, s_pair[s, pair, :, here], preferred_element_type=jnp.float32
                )
                base = decay_state * (both[:8] + both[8:])
                within = jnp.zeros((8, D_HEAD), jnp.float32)
                for back in range(STEPS):
                    b_back = pltpu.roll(b, back, 0) if back else b
                    c_back = pltpu.roll(c, back, 0) if back else c
                    mix = jnp.sum(a * b_back, axis=1, keepdims=True)
                    term = mix * c_back * jnp.exp(-slope * float(back))
                    late = (step >= BEFORE) & (step < STEPS)
                    if back < BEFORE:
                        keep = ((step < BEFORE) & (step >= back)) | (late & (step >= BEFORE + back))
                        within = within + jnp.where(keep, term, 0.0)
                    if back:
                        cross = late & (step >= back) & (step < BEFORE + back)
                        base = base + jnp.where(cross, term, 0.0)
                base_v[s, :, cols] = base
                w_v[s, :, cols] = within
        return carry

    lax.fori_loop(0, heads // 2, own, 0)

    def answer(j):
        q = q_in[j, 0:rows]
        high, low = split(q)
        left = jnp.concatenate([high, low], axis=0)
        left = jnp.concatenate([left, left], axis=1).astype(jnp.bfloat16)
        total = jnp.zeros((rows, D_HEAD), jnp.float32)
        for pair in range(per_hub // 2):
            both = jnp.dot(
                left, s_pair[moving, j * (per_hub // 2) + pair], preferred_element_type=jnp.float32
            )
            both = both[:rows] + both[rows:]
            for side in range(2):
                total = jnp.where(
                    piece_head == 2 * pair + side,
                    both[:, side * D_HEAD : (side + 1) * D_HEAD],
                    total,
                )
        total = total * fade[j, 0]
        for s in range(BEFORE):
            mix = jnp.sum(q * early_k[s, j, 0:rows], axis=1, keepdims=True)
            total = total + mix * early_v[s, j, 0:rows] * fade[j, 1 + s]
        r_out[j, 0:rows] = total

    turn = jnp.where(me >= count // 2, max(1, hubs // 2), 0)

    def reply(jj, carry):
        j = lax.rem(turn + jj, hubs)

        @pl.when(hub_at(j) != me)
        def _():
            arrive(q_in.at[j, 0:rows], recv_b.at[j])

        answer(j)

        @pl.when(hub_at(j) != me)
        def _():
            to_hub_back(j).start()

        return carry

    lax.fori_loop(0, hubs, reply, 0)

    @pl.when(is_hub)
    def _():
        hub_r[me] = r_out[hub_rank]

    loads[5].wait()
    loads[6].wait()
    rows_of(g_v, scale_v)
    for s in range(slots):
        gate = scale_v[s, 0:STEPS, :]
        scale_v[s, 0:STEPS, :] = gain_v[...] / (1.0 + jnp.exp(-gate))
        scale_v[s, STEPS:, :] = jnp.zeros((8 - STEPS, width), jnp.float32)
    for s in range(slots):
        mixed = base_v[s] + w_v[s]
        energy = jnp.sum(mixed * mixed, axis=1, keepdims=True) * (1.0 / width)
        row = mixed * lax.rsqrt(energy + 1e-06) * scale_v[s]
        for t in range(STEPS):
            row_v[t, s : s + 1, :] = row[t : t + 1]
    for t in range(BEFORE):
        out_ref[t] = row_v[t].astype(out_ref.dtype)

    @pl.when(is_hub)
    def _():
        def gather(k, carry):
            arrive(hub_r.at[other(k), 0:rows], recv_c.at[other(k)])
            return carry

        lax.fori_loop(1, count, gather, 0)

        def choose(i):
            place = jnp.full((1, D_HEAD), i, jnp.int32).astype(jnp.float32)
            chosen = hub_r[0, 0:rows]
            for e in range(1, count):
                chosen = jnp.where(hub_in[e, rows : rows + 1, :] == place, hub_r[e, 0:rows], chosen)
            return chosen

        def back(k, carry):
            i = in_turn(k)
            hub_f[i, 0:rows] = choose(i)
            from_hub_back(i).start()
            return carry

        lax.fori_loop(0, count - 1, back, 0, unroll=hub_unroll)
        final[pl.ds(final_at, rows), :] = choose(me)

    each_hub(lambda j: to_hub_first(j).wait_send())
    each_hub(lambda j: to_hub_back(j).wait_send())

    each_hub(lambda j: arrive(final.at[pl.ds(LEAD + room * j, rows)], recv_d.at[j]))

    square = jnp.zeros((8, D_HEAD), jnp.float32)
    mixed = []
    for h in range(heads):
        top = LEAD + room * (h // per_hub) + GROUP * (h % per_hub) - BEFORE
        got = final[top : top + 8, :] + w_v[moving, :, h * D_HEAD : (h + 1) * D_HEAD]
        square = square + got * got
        mixed.append(got)
    energy = jnp.sum(square, axis=1, keepdims=True) * (1.0 / width)
    inverse = lax.rsqrt(energy + 1e-06)
    moved = lax.broadcasted_iota(jnp.int32, (slots, D_HEAD), 0) == moving
    for h in range(heads):
        cols = slice(h * D_HEAD, (h + 1) * D_HEAD)
        row = mixed[h] * inverse * scale_v[moving, :, cols]
        for t in range(BEFORE, STEPS):
            value = jnp.where(
                moved, jnp.broadcast_to(row[t : t + 1], (slots, D_HEAD)), row_v[t, :, cols]
            )
            out_ref[t, :, cols] = value.astype(out_ref.dtype)

    @pl.when(is_hub)
    def _():
        def drain(k, carry):
            from_hub_first(other(k)).wait_send()
            from_hub_back(other(k)).wait_send()
            return carry

        lax.fori_loop(1, count, drain, 0)


def on_device(queries, keys, values, gates, states, new_slot, norm_gain):
    queries, keys, values, gates = (x.transpose(1, 0, 2) for x in (queries, keys, values, gates))
    steps, slots, width = queries.shape
    heads = states.shape[1]
    count = lax.axis_size("req")
    hubs = max(1, min(count // 4, heads // 2))
    room = -(-(GROUP * (heads // hubs) + 1) // 8) * 8
    f32, bf16 = jnp.float32, jnp.bfloat16
    hbm = pl.BlockSpec(memory_space=pl.ANY)
    dma = pltpu.SemaphoreType.DMA
    slab = pltpu.VMEM((slots, 8, width), f32)
    return pl.pallas_call(
        functools.partial(kernel, count, hubs),
        out_shape=pltpu.VMEM(queries.shape, queries.dtype),
        in_specs=[hbm] * 7,
        out_specs=pl.BlockSpec(memory_space=pltpu.VMEM),
        scratch_shapes=[
            pltpu.SMEM(new_slot.shape, new_slot.dtype),
            pltpu.VMEM(queries.shape, bf16),
            pltpu.VMEM(queries.shape, bf16),
            pltpu.VMEM(queries.shape, bf16),
            pltpu.VMEM(queries.shape, bf16),
            pltpu.VMEM((1, width), f32),
            pltpu.VMEM(states.shape, f32),
            pltpu.VMEM((slots, heads // 2, 2 * D_HEAD, 2 * D_HEAD), bf16),
            slab,
            slab,
            slab,
            slab,
            slab,
            slab,
            pltpu.VMEM((steps, slots, width), f32),
            pltpu.VMEM((BEFORE, hubs, room, D_HEAD), f32),
            pltpu.VMEM((BEFORE, hubs, room, D_HEAD), f32),
            pltpu.VMEM((hubs, 1 + BEFORE, GROUP * (heads // hubs), D_HEAD), f32),
            pltpu.VMEM((hubs, room, D_HEAD), f32),
            pltpu.VMEM((count, room, D_HEAD), f32),
            pltpu.VMEM((count, room, D_HEAD), f32),
            pltpu.VMEM((hubs, room, D_HEAD), f32),
            pltpu.VMEM((hubs, room, D_HEAD), f32),
            pltpu.VMEM((count, room, D_HEAD), f32),
            pltpu.VMEM((count, room, D_HEAD), f32),
            pltpu.VMEM((LEAD + room * hubs + 8, D_HEAD), f32),
            dma((7,)),
            dma((slots,)),
            dma((hubs,)),
            dma((count,)),
            dma((count,)),
            dma((hubs,)),
            dma((hubs,)),
            dma((count,)),
            dma((count,)),
            dma((hubs,)),
        ],
        compiler_params=pltpu.CompilerParams(collective_id=0, has_side_effects=True),
    )(new_slot, queries, keys, values, gates, norm_gain.reshape(1, width), states).transpose(
        1, 0, 2
    )


def solution(mesh):
    in_specs = (
        P(("groups", "req"), None, None),
        P(("groups", "req"), None, None),
        P(("groups", "req"), None, None),
        P(("groups", "req"), None, None),
        P(("groups", "req"), None, None, None),
        P(("groups", "req")),
        P(),
    )
    out_specs = P(("groups", "req"), None, None)
    return jax.shard_map(
        on_device, mesh=mesh, in_specs=in_specs, out_specs=out_specs, check_vma=False
    )
```

```python
import functools
import math

import jax
import jax.numpy as jnp
from jax import lax
from jax.experimental import pallas as pl
from jax.experimental.pallas import tpu as pltpu
from jax.sharding import PartitionSpec as P

D_HEAD = 128
BEFORE = 3
STEPS = 6
MODEL_HEADS = 64
GROUP = STEPS - BEFORE
LEAD = 8

MESH = pl.DeviceIdType.MESH


def silu(x):
    return x / (1.0 + jnp.exp(-x))


def split(x):
    high = x.astype(jnp.bfloat16).astype(jnp.float32)
    return high, x - high


def rows_of(src, dst):
    for t in range(STEPS):
        both = src[t].astype(jnp.float32)
        for s in range(both.shape[0]):
            dst[s, t : t + 1, :] = both[s : s + 1]


def head_slope(heads):
    return jnp.exp((heads + 1.0) * (-8.0 / MODEL_HEADS * math.log(2.0)))


def kernel(
    count,
    hubs,
    slot_hbm,
    q_hbm,
    k_hbm,
    v_hbm,
    g_hbm,
    gain_hbm,
    s_hbm,
    out_ref,
    slot_ref,
    q_v,
    k_v,
    v_v,
    g_v,
    gain_v,
    s_v,
    s_pair,
    a_v,
    b_v,
    c_v,
    w_v,
    base_v,
    scale_v,
    row_v,
    early_k,
    early_v,
    fade,
    piece,
    hub_in,
    hub_out,
    q_in,
    r_out,
    hub_r,
    hub_f,
    final,
    load_sem,
    state_sem,
    send_a,
    recv_a,
    send_b,
    recv_b,
    send_c,
    recv_c,
    send_d,
    recv_d,
):
    slots, heads = s_hbm.shape[0], s_hbm.shape[1]
    width = heads * D_HEAD
    per_hub = heads // hubs
    rows = GROUP * per_hub
    room = piece.shape[1]
    full = fade.shape[2]
    first = count // 2 - hubs
    me = lax.axis_index("req")
    is_hub = (me >= first) & (me < first + 2 * hubs) & (lax.rem(me, 2) == 1)
    hub_rank = jnp.clip(me - first, 0, 2 * hubs - 1) // 2

    def hub_at(j):
        return first + 2 * j + 1

    loads = [
        pltpu.make_async_copy(src, dst, load_sem.at[k])
        for k, (src, dst) in enumerate(
            (
                (slot_hbm, slot_ref),
                (q_hbm.at[BEFORE:], q_v.at[BEFORE:]),
                (q_hbm.at[:BEFORE], q_v.at[:BEFORE]),
                (k_hbm, k_v),
                (v_hbm, v_v),
                (g_hbm, g_v),
                (gain_hbm, gain_v),
            )
        )
    ]
    state_loads = [
        pltpu.make_async_copy(s_hbm.at[s], s_v.at[s], state_sem.at[s]) for s in range(slots)
    ]
    loads[0].start()
    loads[1].start()

    barrier = pltpu.get_barrier_semaphore()

    def other(k):
        return lax.rem(me + k, count)

    @pl.when(is_hub)
    def _():
        def greet(k, carry):
            pl.semaphore_signal(barrier, inc=1, device_id={"req": other(k)}, device_id_type=MESH)
            return carry

        lax.fori_loop(1, count, greet, 0, unroll=5 if (count - 1) % 5 == 0 else 1)

    for copy in loads[2:5] + state_loads + loads[5:]:
        copy.start()

    loads[0].wait()
    moving = jnp.int32(0)
    for s in range(slots):
        moving = jnp.where(slot_ref[s] != me * slots + s, jnp.int32(s), moving)
    wanted = slot_ref[moving] // slots
    wanted_row = jnp.full((1, D_HEAD), wanted, jnp.int32).astype(jnp.float32)

    loads[1].wait()
    span = per_hub * D_HEAD

    def pack(j, carry):
        cols = pl.ds(pl.multiple_of(j * span, D_HEAD), span)
        for t in range(GROUP):
            both = q_v[BEFORE + t, :, cols].astype(jnp.float32)
            raw = both[0:1]
            for s in range(1, slots):
                raw = jnp.where(moving == s, both[s : s + 1], raw)
            for hh in range(per_hub):
                row = GROUP * hh + t
                piece[j, row : row + 1, :] = raw[:, hh * D_HEAD : (hh + 1) * D_HEAD]
        piece[j, 0:rows, :] = silu(piece[j, 0:rows, :])
        piece[j, rows : rows + 1, :] = wanted_row
        return carry

    lax.fori_loop(0, hubs, pack, 0)

    @pl.when(is_hub)
    def _():
        hub_in[me] = piece[hub_rank]

    @pl.when(is_hub)
    def _():
        if hubs > 1:
            pl.semaphore_wait(barrier, hubs - 1)

    @pl.when(jnp.logical_not(is_hub))
    def _():
        pl.semaphore_wait(barrier, hubs)

    def remote(src, dst, send, recv, target):
        return pltpu.make_async_remote_copy(
            src_ref=src,
            dst_ref=dst,
            send_sem=send,
            recv_sem=recv,
            device_id={"req": target},
            device_id_type=MESH,
        )

    def arrive(dst, recv):
        pltpu.make_async_copy(dst, dst, recv).wait()

    def each_hub(act):
        for j in range(hubs):

            @pl.when(hub_at(j) != me)
            def _():
                act(j)

    def to_hub_first(j):
        return remote(
            piece.at[j, 0 : rows + 1],
            hub_in.at[me, 0 : rows + 1],
            send_a.at[j],
            recv_a.at[me],
            hub_at(j),
        )

    def to_hub_back(j):
        return remote(
            r_out.at[j, 0:rows], hub_r.at[me, 0:rows], send_c.at[j], recv_c.at[me], hub_at(j)
        )

    def from_hub_first(i):
        return remote(
            hub_out.at[i, 0:rows], q_in.at[hub_rank, 0:rows], send_b.at[i], recv_b.at[hub_rank], i
        )

    final_at = pl.multiple_of(LEAD + room * hub_rank, 8)

    def from_hub_back(i):
        return remote(
            hub_f.at[i, 0:rows],
            final.at[pl.ds(final_at, rows)],
            send_d.at[i],
            recv_d.at[hub_rank],
            i,
        )

    far = jnp.where(me >= count // 2, 0, max(1, hubs // 2))
    for jj in range(hubs):
        far_j = lax.rem(far + jj, hubs)

        @pl.when(hub_at(far_j) != me)
        def _():
            to_hub_first(far_j).start()

    loads[2].wait()
    rows_of(q_v, a_v)
    for s in range(slots):
        a_v[s, 0:STEPS, :] = silu(a_v[s, 0:STEPS, :])
        a_v[s, STEPS:, :] = jnp.zeros((8 - STEPS, width), jnp.float32)
    loads[3].wait()
    loads[4].wait()
    rows_of(k_v, b_v)
    rows_of(v_v, c_v)
    for s in range(slots):
        b_v[s, 0:STEPS, :] = silu(b_v[s, 0:STEPS, :])
        c_v[s, 0:STEPS, :] = silu(c_v[s, 0:STEPS, :])
        b_v[s, STEPS:, :] = jnp.zeros((8 - STEPS, width), jnp.float32)
        c_v[s, STEPS:, :] = jnp.zeros((8 - STEPS, width), jnp.float32)

    for copy in state_loads:
        copy.wait()

    def halve(h, carry):
        for s in range(slots):
            for side in range(2):
                cols = slice(side * D_HEAD, (side + 1) * D_HEAD)
                high, low = split(s_v[s, 2 * h + side])
                s_pair[s, h, 0:D_HEAD, cols] = high.astype(jnp.bfloat16)
                s_pair[s, h, D_HEAD:, cols] = low.astype(jnp.bfloat16)
        return carry

    lax.fori_loop(0, heads // 2, halve, 0)

    planes = count // hubs
    near = planes // 2 - 1
    order = sorted(range(planes), key=lambda p: (-abs(p - near), -p))
    own_plane = me // hubs
    own_lane = lax.rem(me, hubs)

    def far_first(k):
        place = k // hubs
        plane = order[-1]
        for p in range(planes - 1):
            plane = jnp.where(place == p, order[p], plane)
        plane = jnp.where(own_plane == near, plane, planes - 1 - plane)
        lane = own_lane + lax.rem(k, hubs) + jnp.where(plane == own_plane, 1, 0)
        return plane * hubs + lax.rem(lane, hubs)

    def in_turn(k):
        return k + jnp.where(k >= me, 1, 0)

    hub_unroll = 5 if (count - 1) % 5 == 0 else 1

    @pl.when(is_hub)
    def _():
        def gather(k, carry):
            arrive(hub_in.at[other(k), 0 : rows + 1], recv_a.at[other(k)])
            return carry

        lax.fori_loop(1, count, gather, 0)

        def choose(i):
            want = hub_in[i, rows : rows + 1, :]
            chosen = hub_in[0, 0:rows]
            for e in range(1, count):
                chosen = jnp.where(want == float(e), hub_in[e, 0:rows], chosen)
            return chosen

        def hand(k, carry):
            i = far_first(k)
            hub_out[i, 0:rows] = choose(i)
            from_hub_first(i).start()
            return carry

        lax.fori_loop(0, count - 1, hand, 0, unroll=hub_unroll)
        q_in[hub_rank, 0:rows] = choose(me)

    piece_row = lax.broadcasted_iota(jnp.int32, (full, D_HEAD), 0)
    piece_head = jnp.zeros((full, D_HEAD), jnp.int32)
    for hh in range(1, per_hub):
        piece_head = jnp.where(piece_row >= GROUP * hh, hh, piece_head)
    piece_step = (piece_row - GROUP * piece_head).astype(jnp.float32)
    def fading(j, carry):
        slope = head_slope((piece_head + j * per_hub).astype(jnp.float32))
        fade[j, 0] = jnp.exp(-slope * (piece_step + (BEFORE + 1.0)))
        for s in range(BEFORE):
            fade[j, 1 + s] = jnp.exp(-slope * (piece_step + float(BEFORE - s)))
        return carry

    lax.fori_loop(0, hubs, fading, 0)
    for h in range(heads):
        j, hh = divmod(h, per_hub)
        cols = slice(h * D_HEAD, (h + 1) * D_HEAD)
        for s in range(BEFORE):
            early_k[s, j, GROUP * hh : GROUP * (hh + 1), :] = jnp.broadcast_to(
                b_v[moving, s : s + 1, cols], (GROUP, D_HEAD)
            )
            early_v[s, j, GROUP * hh : GROUP * (hh + 1), :] = jnp.broadcast_to(
                c_v[moving, s : s + 1, cols], (GROUP, D_HEAD)
            )

    step = lax.broadcasted_iota(jnp.int32, (8, D_HEAD), 0)
    step_f = step.astype(jnp.float32)

    def owns(*parts):
        def own(pair, carry):
            for s in range(slots):
                wide = pl.ds(pl.multiple_of(pair * 2 * D_HEAD, D_HEAD), 2 * D_HEAD)
                a_high, a_low = split(a_v[s, :, wide])
                left = jnp.concatenate(
                    [x[:, k * D_HEAD : (k + 1) * D_HEAD] for k in range(2) for x in (a_high, a_low)],
                    axis=0,
                )
                left = jnp.concatenate([left, left], axis=1).astype(jnp.bfloat16)
                pltpu.matmul_push_rhs(s_pair[s, pair], 0, s % 2)
                pltpu.matmul_acc_lhs(parts[s % 2], left, load_staged_rhs=0)
                product = pltpu.matmul_pop(parts[s % 2])
                for side in range(2):
                    h = 2 * pair + side
                    here = slice(side * D_HEAD, (side + 1) * D_HEAD)
                    cols = pl.ds(pl.multiple_of(h * D_HEAD, D_HEAD), D_HEAD)
                    slope = head_slope(jnp.full((8, D_HEAD), h, jnp.int32).astype(jnp.float32))
                    decay_state = jnp.exp(-slope * (step_f + 1.0))
                    a, b, c = a_v[s, :, cols], b_v[s, :, cols], c_v[s, :, cols]
                    both = product[16 * side : 16 * (side + 1), here]
                    base = decay_state * (both[:8] + both[8:])
                    within = jnp.zeros((8, D_HEAD), jnp.float32)
                    for back in range(STEPS):
                        b_back = pltpu.roll(b, back, 0) if back else b
                        c_back = pltpu.roll(c, back, 0) if back else c
                        mix = jnp.sum(a * b_back, axis=1, keepdims=True)
                        term = mix * c_back * jnp.exp(-slope * float(back))
                        late = (step >= BEFORE) & (step < STEPS)
                        if back < BEFORE:
                            keep = ((step < BEFORE) & (step >= back)) | (late & (step >= BEFORE + back))
                            within = within + jnp.where(keep, term, 0.0)
                        if back:
                            cross = late & (step >= back) & (step < BEFORE + back)
                            base = base + jnp.where(cross, term, 0.0)
                    base_v[s, :, cols] = base
                    w_v[s, :, cols] = within
            return carry

        lax.fori_loop(0, heads // 2, own, 0)

    pl.run_scoped(owns, *(pltpu.ACC(mxu_id=k)((32, 2 * D_HEAD), jnp.float32) for k in range(2)))

    pairs = per_hub // 2
    staged = min(4, pairs)

    def stage(j, begin):
        for k in range(min(staged, pairs - begin)):
            pltpu.matmul_push_rhs(s_pair[moving, j * pairs + begin + k], k // 2, k % 2)

    def replies(*sums):
        def answer(j):
            q = q_in[j, 0:full]
            high, low = split(q)
            left = jnp.concatenate([high, low], axis=0)
            left = jnp.concatenate([left, left], axis=1).astype(jnp.bfloat16)
            total = jnp.zeros((full, D_HEAD), jnp.float32)
            for begin in range(0, pairs, staged):
                if begin:
                    stage(j, begin)
                for k in range(min(staged, pairs - begin)):
                    pltpu.matmul_acc_lhs(sums[k], left, load_staged_rhs=k // 2)
                for k in range(min(staged, pairs - begin)):
                    both = pltpu.matmul_pop(sums[k])
                    both = both[:full] + both[full:]
                    for side in range(2):
                        total = jnp.where(
                            piece_head == 2 * (begin + k) + side,
                            both[:, side * D_HEAD : (side + 1) * D_HEAD],
                            total,
                        )
            total = total * fade[j, 0]
            for s in range(BEFORE):
                mix = jnp.sum(q * early_k[s, j, 0:full], axis=1, keepdims=True)
                total = total + mix * early_v[s, j, 0:full] * fade[j, 1 + s]
            r_out[j, 0:full] = total

        turn = jnp.where(me >= count // 2, max(1, hubs // 2), 0)

        def reply(jj, carry):
            j = lax.rem(turn + jj, hubs)
            stage(j, 0)

            @pl.when(hub_at(j) != me)
            def _():
                arrive(q_in.at[j, 0:rows], recv_b.at[j])

            answer(j)

            @pl.when(hub_at(j) != me)
            def _():
                to_hub_back(j).start()

            return carry

        lax.fori_loop(0, hubs, reply, 0)

    pl.run_scoped(
        replies,
        *(pltpu.ACC(mxu_id=k % 2)((2 * full, 2 * D_HEAD), jnp.float32) for k in range(staged)),
    )

    @pl.when(is_hub)
    def _():
        hub_r[me] = r_out[hub_rank]

    loads[5].wait()
    loads[6].wait()
    rows_of(g_v, scale_v)
    for s in range(slots):
        gate = scale_v[s, 0:STEPS, :]
        scale_v[s, 0:STEPS, :] = gain_v[...] / (1.0 + jnp.exp(-gate))
        scale_v[s, STEPS:, :] = jnp.zeros((8 - STEPS, width), jnp.float32)
    for s in range(slots):
        mixed = base_v[s] + w_v[s]
        energy = jnp.sum(mixed * mixed, axis=1, keepdims=True) * (1.0 / width)
        row = mixed * lax.rsqrt(energy + 1e-06) * scale_v[s]
        for t in range(STEPS):
            row_v[t, s : s + 1, :] = row[t : t + 1]
    for t in range(BEFORE):
        out_ref[t] = row_v[t].astype(out_ref.dtype)

    @pl.when(is_hub)
    def _():
        def gather(k, carry):
            arrive(hub_r.at[other(k), 0:rows], recv_c.at[other(k)])
            return carry

        lax.fori_loop(1, count, gather, 0)

        def choose(i):
            place = jnp.full((1, D_HEAD), i, jnp.int32).astype(jnp.float32)
            chosen = hub_r[0, 0:rows]
            for e in range(1, count):
                chosen = jnp.where(hub_in[e, rows : rows + 1, :] == place, hub_r[e, 0:rows], chosen)
            return chosen

        def back(k, carry):
            i = in_turn(k)
            hub_f[i, 0:rows] = choose(i)
            from_hub_back(i).start()
            return carry

        lax.fori_loop(0, count - 1, back, 0, unroll=hub_unroll)
        final[pl.ds(final_at, rows), :] = choose(me)

    each_hub(lambda j: to_hub_first(j).wait_send())
    each_hub(lambda j: to_hub_back(j).wait_send())

    each_hub(lambda j: arrive(final.at[pl.ds(LEAD + room * j, rows)], recv_d.at[j]))

    square = jnp.zeros((8, D_HEAD), jnp.float32)
    mixed = []
    for h in range(heads):
        top = LEAD + room * (h // per_hub) + GROUP * (h % per_hub) - BEFORE
        got = final[top : top + 8, :] + w_v[moving, :, h * D_HEAD : (h + 1) * D_HEAD]
        square = square + got * got
        mixed.append(got)
    energy = jnp.sum(square, axis=1, keepdims=True) * (1.0 / width)
    inverse = lax.rsqrt(energy + 1e-06)
    moved = lax.broadcasted_iota(jnp.int32, (slots, D_HEAD), 0) == moving
    for h in range(heads):
        cols = slice(h * D_HEAD, (h + 1) * D_HEAD)
        row = mixed[h] * inverse * scale_v[moving, :, cols]
        for t in range(BEFORE, STEPS):
            value = jnp.where(
                moved, jnp.broadcast_to(row[t : t + 1], (slots, D_HEAD)), row_v[t, :, cols]
            )
            out_ref[t, :, cols] = value.astype(out_ref.dtype)

    @pl.when(is_hub)
    def _():
        def drain(k, carry):
            from_hub_first(other(k)).wait_send()
            from_hub_back(other(k)).wait_send()
            return carry

        lax.fori_loop(1, count, drain, 0)


def on_device(queries, keys, values, gates, states, new_slot, norm_gain):
    queries, keys, values, gates = (x.transpose(1, 0, 2) for x in (queries, keys, values, gates))
    steps, slots, width = queries.shape
    heads = states.shape[1]
    count = lax.axis_size("req")
    hubs = max(1, min(count // 4, heads // 2))
    room = -(-(GROUP * (heads // hubs) + 1) // 8) * 8
    f32, bf16 = jnp.float32, jnp.bfloat16
    hbm = pl.BlockSpec(memory_space=pl.ANY)
    dma = pltpu.SemaphoreType.DMA
    slab = pltpu.VMEM((slots, 8, width), f32)
    return pl.pallas_call(
        functools.partial(kernel, count, hubs),
        out_shape=pltpu.VMEM(queries.shape, queries.dtype),
        in_specs=[hbm] * 7,
        out_specs=pl.BlockSpec(memory_space=pltpu.VMEM),
        scratch_shapes=[
            pltpu.SMEM(new_slot.shape, new_slot.dtype),
            pltpu.VMEM(queries.shape, bf16),
            pltpu.VMEM(queries.shape, bf16),
            pltpu.VMEM(queries.shape, bf16),
            pltpu.VMEM(queries.shape, bf16),
            pltpu.VMEM((1, width), f32),
            pltpu.VMEM(states.shape, f32),
            pltpu.VMEM((slots, heads // 2, 2 * D_HEAD, 2 * D_HEAD), bf16),
            slab,
            slab,
            slab,
            slab,
            slab,
            slab,
            pltpu.VMEM((steps, slots, width), f32),
            pltpu.VMEM((BEFORE, hubs, room, D_HEAD), f32),
            pltpu.VMEM((BEFORE, hubs, room, D_HEAD), f32),
            pltpu.VMEM((hubs, 1 + BEFORE, -(-GROUP * (heads // hubs) // 8) * 8, D_HEAD), f32),
            pltpu.VMEM((hubs, room, D_HEAD), f32),
            pltpu.VMEM((count, room, D_HEAD), f32),
            pltpu.VMEM((count, room, D_HEAD), f32),
            pltpu.VMEM((hubs, room, D_HEAD), f32),
            pltpu.VMEM((hubs, room, D_HEAD), f32),
            pltpu.VMEM((count, room, D_HEAD), f32),
            pltpu.VMEM((count, room, D_HEAD), f32),
            pltpu.VMEM((LEAD + room * hubs + 8, D_HEAD), f32),
            dma((7,)),
            dma((slots,)),
            dma((hubs,)),
            dma((count,)),
            dma((count,)),
            dma((hubs,)),
            dma((hubs,)),
            dma((count,)),
            dma((count,)),
            dma((hubs,)),
        ],
        compiler_params=pltpu.CompilerParams(collective_id=0, has_side_effects=True),
    )(new_slot, queries, keys, values, gates, norm_gain.reshape(1, width), states).transpose(
        1, 0, 2
    )


def solution(mesh):
    in_specs = (
        P(("groups", "req"), None, None),
        P(("groups", "req"), None, None),
        P(("groups", "req"), None, None),
        P(("groups", "req"), None, None),
        P(("groups", "req"), None, None, None),
        P(("groups", "req")),
        P(),
    )
    out_specs = P(("groups", "req"), None, None)
    return jax.shard_map(
        on_device, mesh=mesh, in_specs=in_specs, out_specs=out_specs, check_vma=False
    )
```

```python
import functools
import math

import jax
import jax.numpy as jnp
from jax import lax
from jax.experimental import pallas as pl
from jax.experimental.pallas import tpu as pltpu
from jax.sharding import PartitionSpec as P

D_HEAD = 128
BEFORE = 3
STEPS = 6
MODEL_HEADS = 64
GROUP = STEPS - BEFORE
LEAD = 8

MESH = pl.DeviceIdType.MESH


def silu(x):
    return x / (1.0 + jnp.exp(-x))


def split(x):
    high = x.astype(jnp.bfloat16).astype(jnp.float32)
    return high, x - high


def rows_of(src, dst):
    for t in range(STEPS):
        both = src[t].astype(jnp.float32)
        for s in range(both.shape[0]):
            dst[s, t : t + 1, :] = both[s : s + 1]


def head_slope(heads):
    return jnp.exp((heads + 1.0) * (-8.0 / MODEL_HEADS * math.log(2.0)))


def kernel(
    count,
    hubs,
    slot_hbm,
    q_hbm,
    k_hbm,
    v_hbm,
    g_hbm,
    gain_hbm,
    s_hbm,
    out_ref,
    slot_ref,
    q_v,
    k_v,
    v_v,
    g_v,
    gain_v,
    s_v,
    s_pair,
    a_v,
    b_v,
    c_v,
    w_v,
    base_v,
    scale_v,
    row_v,
    early_k,
    early_v,
    fade,
    piece,
    hub_in,
    hub_out,
    q_in,
    r_out,
    hub_r,
    hub_f,
    final,
    load_sem,
    state_sem,
    send_a,
    recv_a,
    send_b,
    recv_b,
    send_c,
    recv_c,
    send_d,
    recv_d,
):
    slots, heads = s_hbm.shape[0], s_hbm.shape[1]
    width = heads * D_HEAD
    per_hub = heads // hubs
    rows = GROUP * per_hub
    room = piece.shape[1]
    full = fade.shape[2]
    first = count // 2 - hubs
    me = lax.axis_index("req")
    is_hub = (me >= first) & (me < first + 2 * hubs) & (lax.rem(me, 2) == 1)
    hub_rank = jnp.clip(me - first, 0, 2 * hubs - 1) // 2

    def hub_at(j):
        return first + 2 * j + 1

    loads = [
        pltpu.make_async_copy(src, dst, load_sem.at[k])
        for k, (src, dst) in enumerate(
            (
                (slot_hbm, slot_ref),
                (q_hbm.at[BEFORE:], q_v.at[BEFORE:]),
                (q_hbm.at[:BEFORE], q_v.at[:BEFORE]),
                (k_hbm, k_v),
                (v_hbm, v_v),
                (g_hbm, g_v),
                (gain_hbm, gain_v),
            )
        )
    ]
    state_loads = [
        pltpu.make_async_copy(s_hbm.at[s], s_v.at[s], state_sem.at[s]) for s in range(slots)
    ]
    loads[0].start()
    loads[1].start()

    barrier = pltpu.get_barrier_semaphore()

    def other(k):
        return lax.rem(me + k, count)

    @pl.when(is_hub)
    def _():
        def greet(k, carry):
            pl.semaphore_signal(barrier, inc=1, device_id={"req": other(k)}, device_id_type=MESH)
            return carry

        lax.fori_loop(1, count, greet, 0, unroll=5 if (count - 1) % 5 == 0 else 1)

    for copy in loads[2:5] + state_loads + loads[5:]:
        copy.start()

    loads[0].wait()
    moving = jnp.int32(0)
    for s in range(slots):
        moving = jnp.where(slot_ref[s] != me * slots + s, jnp.int32(s), moving)
    wanted = slot_ref[moving] // slots
    wanted_row = jnp.full((1, D_HEAD), wanted, jnp.int32).astype(jnp.float32)

    loads[1].wait()
    span = per_hub * D_HEAD

    def pack(j, carry):
        cols = pl.ds(pl.multiple_of(j * span, D_HEAD), span)
        for t in range(GROUP):
            both = q_v[BEFORE + t, :, cols].astype(jnp.float32)
            raw = both[0:1]
            for s in range(1, slots):
                raw = jnp.where(moving == s, both[s : s + 1], raw)
            for hh in range(per_hub):
                row = GROUP * hh + t
                piece[j, row : row + 1, :] = raw[:, hh * D_HEAD : (hh + 1) * D_HEAD]
        piece[j, 0:rows, :] = silu(piece[j, 0:rows, :])
        piece[j, rows : rows + 1, :] = wanted_row
        return carry

    lax.fori_loop(0, hubs, pack, 0)

    @pl.when(is_hub)
    def _():
        hub_in[me] = piece[hub_rank]

    @pl.when(is_hub)
    def _():
        if hubs > 1:
            pl.semaphore_wait(barrier, hubs - 1)

    @pl.when(jnp.logical_not(is_hub))
    def _():
        pl.semaphore_wait(barrier, hubs)

    def remote(src, dst, send, recv, target):
        return pltpu.make_async_remote_copy(
            src_ref=src,
            dst_ref=dst,
            send_sem=send,
            recv_sem=recv,
            device_id={"req": target},
            device_id_type=MESH,
        )

    def arrive(dst, recv):
        pltpu.make_async_copy(dst, dst, recv).wait()

    def each_hub(act):
        for j in range(hubs):

            @pl.when(hub_at(j) != me)
            def _():
                act(j)

    def to_hub_first(j):
        return remote(
            piece.at[j, 0 : rows + 1],
            hub_in.at[me, 0 : rows + 1],
            send_a.at[j],
            recv_a.at[me],
            hub_at(j),
        )

    def to_hub_back(j):
        return remote(
            r_out.at[j, 0:rows], hub_r.at[me, 0:rows], send_c.at[j], recv_c.at[me], hub_at(j)
        )

    def from_hub_first(i):
        return remote(
            hub_out.at[i, 0:rows], q_in.at[hub_rank, 0:rows], send_b.at[i], recv_b.at[hub_rank], i
        )

    final_at = pl.multiple_of(LEAD + room * hub_rank, 8)

    def from_hub_back(i):
        return remote(
            hub_f.at[i, 0:rows],
            final.at[pl.ds(final_at, rows)],
            send_d.at[i],
            recv_d.at[hub_rank],
            i,
        )

    far = jnp.where(me >= count // 2, 0, max(1, hubs // 2))
    for jj in range(hubs):
        far_j = lax.rem(far + jj, hubs)

        @pl.when(hub_at(far_j) != me)
        def _():
            to_hub_first(far_j).start()

    loads[2].wait()
    rows_of(q_v, a_v)
    for s in range(slots):
        a_v[s, 0:STEPS, :] = silu(a_v[s, 0:STEPS, :])
        a_v[s, STEPS:, :] = jnp.zeros((8 - STEPS, width), jnp.float32)
    loads[3].wait()
    loads[4].wait()
    rows_of(k_v, b_v)
    rows_of(v_v, c_v)
    for s in range(slots):
        b_v[s, 0:STEPS, :] = silu(b_v[s, 0:STEPS, :])
        c_v[s, 0:STEPS, :] = silu(c_v[s, 0:STEPS, :])
        b_v[s, STEPS:, :] = jnp.zeros((8 - STEPS, width), jnp.float32)
        c_v[s, STEPS:, :] = jnp.zeros((8 - STEPS, width), jnp.float32)

    for copy in state_loads:
        copy.wait()

    def halve(h, carry):
        for s in range(slots):
            for side in range(2):
                cols = slice(side * D_HEAD, (side + 1) * D_HEAD)
                high, low = split(s_v[s, 2 * h + side])
                s_pair[s, h, 0:D_HEAD, cols] = high.astype(jnp.bfloat16)
                s_pair[s, h, D_HEAD:, cols] = low.astype(jnp.bfloat16)
        return carry

    lax.fori_loop(0, heads // 2, halve, 0)

    planes = count // hubs
    near = planes // 2 - 1
    order = sorted(range(planes), key=lambda p: (-abs(p - near), -p))
    own_plane = me // hubs
    own_lane = lax.rem(me, hubs)

    def far_first(k):
        place = k // hubs
        plane = order[-1]
        for p in range(planes - 1):
            plane = jnp.where(place == p, order[p], plane)
        plane = jnp.where(own_plane == near, plane, planes - 1 - plane)
        lane = own_lane + lax.rem(k, hubs) + jnp.where(plane == own_plane, 1, 0)
        return plane * hubs + lax.rem(lane, hubs)

    def in_turn(k):
        return k + jnp.where(k >= me, 1, 0)

    hub_unroll = 5 if (count - 1) % 5 == 0 else 1

    @pl.when(is_hub)
    def _():
        def gather(k, carry):
            arrive(hub_in.at[other(k), 0 : rows + 1], recv_a.at[other(k)])
            return carry

        lax.fori_loop(1, count, gather, 0)

        def choose(i):
            want = hub_in[i, rows : rows + 1, :]
            chosen = hub_in[0, 0:rows]
            for e in range(1, count):
                chosen = jnp.where(want == float(e), hub_in[e, 0:rows], chosen)
            return chosen

        def hand(k, carry):
            i = jnp.where(own_plane == near, count - 1 - (k + jnp.where(k >= count - 1 - me, 1, 0)), in_turn(k))
            hub_out[i, 0:rows] = choose(i)
            from_hub_first(i).start()
            return carry

        lax.fori_loop(0, count - 1, hand, 0, unroll=hub_unroll)
        q_in[hub_rank, 0:rows] = choose(me)

    piece_row = lax.broadcasted_iota(jnp.int32, (full, D_HEAD), 0)
    piece_head = jnp.zeros((full, D_HEAD), jnp.int32)
    for hh in range(1, per_hub):
        piece_head = jnp.where(piece_row >= GROUP * hh, hh, piece_head)
    piece_step = (piece_row - GROUP * piece_head).astype(jnp.float32)
    def fading(j, carry):
        slope = head_slope((piece_head + j * per_hub).astype(jnp.float32))
        fade[j, 0] = jnp.exp(-slope * (piece_step + (BEFORE + 1.0)))
        for s in range(BEFORE):
            fade[j, 1 + s] = jnp.exp(-slope * (piece_step + float(BEFORE - s)))
        return carry

    lax.fori_loop(0, hubs, fading, 0)
    for h in range(heads):
        j, hh = divmod(h, per_hub)
        cols = slice(h * D_HEAD, (h + 1) * D_HEAD)
        for s in range(BEFORE):
            early_k[s, j, GROUP * hh : GROUP * (hh + 1), :] = jnp.broadcast_to(
                b_v[moving, s : s + 1, cols], (GROUP, D_HEAD)
            )
            early_v[s, j, GROUP * hh : GROUP * (hh + 1), :] = jnp.broadcast_to(
                c_v[moving, s : s + 1, cols], (GROUP, D_HEAD)
            )

    step = lax.broadcasted_iota(jnp.int32, (8, D_HEAD), 0)
    step_f = step.astype(jnp.float32)

    def owns(*parts):
        def own(pair, carry):
            for s in range(slots):
                wide = pl.ds(pl.multiple_of(pair * 2 * D_HEAD, D_HEAD), 2 * D_HEAD)
                a_high, a_low = split(a_v[s, :, wide])
                left = jnp.concatenate(
                    [x[:, k * D_HEAD : (k + 1) * D_HEAD] for k in range(2) for x in (a_high, a_low)],
                    axis=0,
                )
                left = jnp.concatenate([left, left], axis=1).astype(jnp.bfloat16)
                pltpu.matmul_push_rhs(s_pair[s, pair], 0, s % 2)
                pltpu.matmul_acc_lhs(parts[s % 2], left, load_staged_rhs=0)
                product = pltpu.matmul_pop(parts[s % 2])
                for side in range(2):
                    h = 2 * pair + side
                    here = slice(side * D_HEAD, (side + 1) * D_HEAD)
                    cols = pl.ds(pl.multiple_of(h * D_HEAD, D_HEAD), D_HEAD)
                    slope = head_slope(jnp.full((8, D_HEAD), h, jnp.int32).astype(jnp.float32))
                    decay_state = jnp.exp(-slope * (step_f + 1.0))
                    a, b, c = a_v[s, :, cols], b_v[s, :, cols], c_v[s, :, cols]
                    both = product[16 * side : 16 * (side + 1), here]
                    base = decay_state * (both[:8] + both[8:])
                    within = jnp.zeros((8, D_HEAD), jnp.float32)
                    for back in range(STEPS):
                        b_back = pltpu.roll(b, back, 0) if back else b
                        c_back = pltpu.roll(c, back, 0) if back else c
                        mix = jnp.sum(a * b_back, axis=1, keepdims=True)
                        term = mix * c_back * jnp.exp(-slope * float(back))
                        late = (step >= BEFORE) & (step < STEPS)
                        if back < BEFORE:
                            keep = ((step < BEFORE) & (step >= back)) | (late & (step >= BEFORE + back))
                            within = within + jnp.where(keep, term, 0.0)
                        if back:
                            cross = late & (step >= back) & (step < BEFORE + back)
                            base = base + jnp.where(cross, term, 0.0)
                    base_v[s, :, cols] = base
                    w_v[s, :, cols] = within
            return carry

        lax.fori_loop(0, heads // 2, own, 0)

    pl.run_scoped(owns, *(pltpu.ACC(mxu_id=k)((32, 2 * D_HEAD), jnp.float32) for k in range(2)))

    pairs = per_hub // 2
    staged = min(4, pairs)

    def stage(j, begin):
        for k in range(min(staged, pairs - begin)):
            pltpu.matmul_push_rhs(s_pair[moving, j * pairs + begin + k], k // 2, k % 2)

    def replies(*sums):
        def answer(j):
            q = q_in[j, 0:full]
            high, low = split(q)
            left = jnp.concatenate([high, low], axis=0)
            left = jnp.concatenate([left, left], axis=1).astype(jnp.bfloat16)
            total = jnp.zeros((full, D_HEAD), jnp.float32)
            for begin in range(0, pairs, staged):
                if begin:
                    stage(j, begin)
                for k in range(min(staged, pairs - begin)):
                    pltpu.matmul_acc_lhs(sums[k], left, load_staged_rhs=k // 2)
                for k in range(min(staged, pairs - begin)):
                    both = pltpu.matmul_pop(sums[k])
                    both = both[:full] + both[full:]
                    for side in range(2):
                        total = jnp.where(
                            piece_head == 2 * (begin + k) + side,
                            both[:, side * D_HEAD : (side + 1) * D_HEAD],
                            total,
                        )
            total = total * fade[j, 0]
            for s in range(BEFORE):
                mix = jnp.sum(q * early_k[s, j, 0:full], axis=1, keepdims=True)
                total = total + mix * early_v[s, j, 0:full] * fade[j, 1 + s]
            r_out[j, 0:full] = total

        turn = jnp.where(me >= count // 2, 0, max(1, hubs // 2))

        def reply(jj, carry):
            j = lax.rem(turn + jj, hubs)
            stage(j, 0)

            @pl.when(hub_at(j) != me)
            def _():
                arrive(q_in.at[j, 0:rows], recv_b.at[j])

            answer(j)

            @pl.when(hub_at(j) != me)
            def _():
                to_hub_back(j).start()

            return carry

        lax.fori_loop(0, hubs, reply, 0)

    pl.run_scoped(
        replies,
        *(pltpu.ACC(mxu_id=k % 2)((2 * full, 2 * D_HEAD), jnp.float32) for k in range(staged)),
    )

    @pl.when(is_hub)
    def _():
        hub_r[me] = r_out[hub_rank]

    loads[5].wait()
    loads[6].wait()
    rows_of(g_v, scale_v)
    for s in range(slots):
        gate = scale_v[s, 0:STEPS, :]
        scale_v[s, 0:STEPS, :] = gain_v[...] / (1.0 + jnp.exp(-gate))
        scale_v[s, STEPS:, :] = jnp.zeros((8 - STEPS, width), jnp.float32)
    for s in range(slots):
        mixed = base_v[s] + w_v[s]
        energy = jnp.sum(mixed * mixed, axis=1, keepdims=True) * (1.0 / width)
        row = mixed * lax.rsqrt(energy + 1e-06) * scale_v[s]
        for t in range(STEPS):
            row_v[t, s : s + 1, :] = row[t : t + 1]
    for t in range(BEFORE):
        out_ref[t] = row_v[t].astype(out_ref.dtype)

    @pl.when(is_hub)
    def _():
        def gather(k, carry):
            arrive(hub_r.at[other(k), 0:rows], recv_c.at[other(k)])
            return carry

        lax.fori_loop(1, count, gather, 0)

        def choose(i):
            place = jnp.full((1, D_HEAD), i, jnp.int32).astype(jnp.float32)
            chosen = hub_r[0, 0:rows]
            for e in range(1, count):
                chosen = jnp.where(hub_in[e, rows : rows + 1, :] == place, hub_r[e, 0:rows], chosen)
            return chosen

        def back(k, carry):
            i = in_turn(k)
            hub_f[i, 0:rows] = choose(i)
            from_hub_back(i).start()
            return carry

        lax.fori_loop(0, count - 1, back, 0, unroll=hub_unroll)
        final[pl.ds(final_at, rows), :] = choose(me)

    each_hub(lambda j: to_hub_first(j).wait_send())
    each_hub(lambda j: to_hub_back(j).wait_send())

    each_hub(lambda j: arrive(final.at[pl.ds(LEAD + room * j, rows)], recv_d.at[j]))

    square = jnp.zeros((8, D_HEAD), jnp.float32)
    mixed = []
    for h in range(heads):
        top = LEAD + room * (h // per_hub) + GROUP * (h % per_hub) - BEFORE
        got = final[top : top + 8, :] + w_v[moving, :, h * D_HEAD : (h + 1) * D_HEAD]
        square = square + got * got
        mixed.append(got)
    energy = jnp.sum(square, axis=1, keepdims=True) * (1.0 / width)
    inverse = lax.rsqrt(energy + 1e-06)
    moved = lax.broadcasted_iota(jnp.int32, (slots, D_HEAD), 0) == moving
    for h in range(heads):
        cols = slice(h * D_HEAD, (h + 1) * D_HEAD)
        row = mixed[h] * inverse * scale_v[moving, :, cols]
        for t in range(BEFORE, STEPS):
            value = jnp.where(
                moved, jnp.broadcast_to(row[t : t + 1], (slots, D_HEAD)), row_v[t, :, cols]
            )
            out_ref[t, :, cols] = value.astype(out_ref.dtype)

    @pl.when(is_hub)
    def _():
        def drain(k, carry):
            from_hub_first(other(k)).wait_send()
            from_hub_back(other(k)).wait_send()
            return carry

        lax.fori_loop(1, count, drain, 0)


def on_device(queries, keys, values, gates, states, new_slot, norm_gain):
    queries, keys, values, gates = (x.transpose(1, 0, 2) for x in (queries, keys, values, gates))
    steps, slots, width = queries.shape
    heads = states.shape[1]
    count = lax.axis_size("req")
    hubs = max(1, min(count // 4, heads // 2))
    room = -(-(GROUP * (heads // hubs) + 1) // 8) * 8
    f32, bf16 = jnp.float32, jnp.bfloat16
    hbm = pl.BlockSpec(memory_space=pl.ANY)
    dma = pltpu.SemaphoreType.DMA
    slab = pltpu.VMEM((slots, 8, width), f32)
    return pl.pallas_call(
        functools.partial(kernel, count, hubs),
        out_shape=pltpu.VMEM(queries.shape, queries.dtype),
        in_specs=[hbm] * 7,
        out_specs=pl.BlockSpec(memory_space=pltpu.VMEM),
        scratch_shapes=[
            pltpu.SMEM(new_slot.shape, new_slot.dtype),
            pltpu.VMEM(queries.shape, bf16),
            pltpu.VMEM(queries.shape, bf16),
            pltpu.VMEM(queries.shape, bf16),
            pltpu.VMEM(queries.shape, bf16),
            pltpu.VMEM((1, width), f32),
            pltpu.VMEM(states.shape, f32),
            pltpu.VMEM((slots, heads // 2, 2 * D_HEAD, 2 * D_HEAD), bf16),
            slab,
            slab,
            slab,
            slab,
            slab,
            slab,
            pltpu.VMEM((steps, slots, width), f32),
            pltpu.VMEM((BEFORE, hubs, room, D_HEAD), f32),
            pltpu.VMEM((BEFORE, hubs, room, D_HEAD), f32),
            pltpu.VMEM((hubs, 1 + BEFORE, -(-GROUP * (heads // hubs) // 8) * 8, D_HEAD), f32),
            pltpu.VMEM((hubs, room, D_HEAD), f32),
            pltpu.VMEM((count, room, D_HEAD), f32),
            pltpu.VMEM((count, room, D_HEAD), f32),
            pltpu.VMEM((hubs, room, D_HEAD), f32),
            pltpu.VMEM((hubs, room, D_HEAD), f32),
            pltpu.VMEM((count, room, D_HEAD), f32),
            pltpu.VMEM((count, room, D_HEAD), f32),
            pltpu.VMEM((LEAD + room * hubs + 8, D_HEAD), f32),
            dma((7,)),
            dma((slots,)),
            dma((hubs,)),
            dma((count,)),
            dma((count,)),
            dma((hubs,)),
            dma((hubs,)),
            dma((count,)),
            dma((count,)),
            dma((hubs,)),
        ],
        compiler_params=pltpu.CompilerParams(collective_id=0, has_side_effects=True),
    )(new_slot, queries, keys, values, gates, norm_gain.reshape(1, width), states).transpose(
        1, 0, 2
    )


def solution(mesh):
    in_specs = (
        P(("groups", "req"), None, None),
        P(("groups", "req"), None, None),
        P(("groups", "req"), None, None),
        P(("groups", "req"), None, None),
        P(("groups", "req"), None, None, None),
        P(("groups", "req")),
        P(),
    )
    out_specs = P(("groups", "req"), None, None)
    return jax.shard_map(
        on_device, mesh=mesh, in_specs=in_specs, out_specs=out_specs, check_vma=False
    )
```

```python
import functools
import math

import jax
import jax.numpy as jnp
from jax import lax
from jax.experimental import pallas as pl
from jax.experimental.pallas import tpu as pltpu
from jax.sharding import PartitionSpec as P

D_HEAD = 128
BEFORE = 3
STEPS = 6
MODEL_HEADS = 64
GROUP = STEPS - BEFORE
LEAD = 8

MESH = pl.DeviceIdType.MESH


def silu(x):
    return x / (1.0 + jnp.exp(-x))


def split(x):
    high = x.astype(jnp.bfloat16).astype(jnp.float32)
    return high, x - high


def rows_of(src, dst):
    for t in range(STEPS):
        both = src[t].astype(jnp.float32)
        for s in range(both.shape[0]):
            dst[s, t : t + 1, :] = both[s : s + 1]


def head_slope(heads):
    return jnp.exp((heads + 1.0) * (-8.0 / MODEL_HEADS * math.log(2.0)))


def kernel(
    count,
    hubs,
    slot_hbm,
    q_hbm,
    k_hbm,
    v_hbm,
    g_hbm,
    gain_hbm,
    s_hbm,
    out_ref,
    slot_ref,
    q_v,
    k_v,
    v_v,
    g_v,
    gain_v,
    s_v,
    s_pair,
    a_v,
    b_v,
    c_v,
    w_v,
    base_v,
    scale_v,
    row_v,
    early_k,
    early_v,
    fade,
    piece,
    hub_in,
    hub_out,
    q_in,
    r_out,
    hub_r,
    hub_f,
    final,
    load_sem,
    state_sem,
    send_a,
    recv_a,
    send_b,
    recv_b,
    send_c,
    recv_c,
    send_d,
    recv_d,
):
    slots, heads = s_hbm.shape[0], s_hbm.shape[1]
    width = heads * D_HEAD
    per_hub = heads // hubs
    rows = GROUP * per_hub
    room = piece.shape[1]
    full = fade.shape[2]
    first = count // 2 - hubs
    me = lax.axis_index("req")
    is_hub = (me >= first) & (me < first + 2 * hubs) & (lax.rem(me, 2) == 1)
    hub_rank = jnp.clip(me - first, 0, 2 * hubs - 1) // 2

    def hub_at(j):
        return first + 2 * j + 1

    loads = [
        pltpu.make_async_copy(src, dst, load_sem.at[k])
        for k, (src, dst) in enumerate(
            (
                (slot_hbm, slot_ref),
                (q_hbm.at[BEFORE:], q_v.at[BEFORE:]),
                (q_hbm.at[:BEFORE], q_v.at[:BEFORE]),
                (k_hbm, k_v),
                (v_hbm, v_v),
                (g_hbm, g_v),
                (gain_hbm, gain_v),
            )
        )
    ]
    state_loads = [
        pltpu.make_async_copy(s_hbm.at[s], s_v.at[s], state_sem.at[s]) for s in range(slots)
    ]
    loads[0].start()
    loads[1].start()

    barrier = pltpu.get_barrier_semaphore()

    def other(k):
        return lax.rem(me + k, count)

    @pl.when(is_hub)
    def _():
        def greet(k, carry):
            pl.semaphore_signal(barrier, inc=1, device_id={"req": other(k)}, device_id_type=MESH)
            return carry

        lax.fori_loop(1, count, greet, 0, unroll=5 if (count - 1) % 5 == 0 else 1)

    for copy in loads[2:5] + state_loads + loads[5:]:
        copy.start()

    loads[0].wait()
    moving = jnp.int32(0)
    for s in range(slots):
        moving = jnp.where(slot_ref[s] != me * slots + s, jnp.int32(s), moving)
    wanted = slot_ref[moving] // slots
    wanted_row = jnp.full((1, D_HEAD), wanted, jnp.int32).astype(jnp.float32)

    loads[1].wait()
    span = per_hub * D_HEAD

    def pack(j, carry):
        cols = pl.ds(pl.multiple_of(j * span, D_HEAD), span)
        for t in range(GROUP):
            both = q_v[BEFORE + t, :, cols].astype(jnp.float32)
            raw = both[0:1]
            for s in range(1, slots):
                raw = jnp.where(moving == s, both[s : s + 1], raw)
            for hh in range(per_hub):
                row = GROUP * hh + t
                piece[j, row : row + 1, :] = raw[:, hh * D_HEAD : (hh + 1) * D_HEAD]
        piece[j, 0:rows, :] = silu(piece[j, 0:rows, :])
        piece[j, rows : rows + 1, :] = wanted_row
        return carry

    lax.fori_loop(0, hubs, pack, 0)

    @pl.when(is_hub)
    def _():
        hub_in[me] = piece[hub_rank]

    @pl.when(is_hub)
    def _():
        if hubs > 1:
            pl.semaphore_wait(barrier, hubs - 1)

    @pl.when(jnp.logical_not(is_hub))
    def _():
        pl.semaphore_wait(barrier, hubs)

    def remote(src, dst, send, recv, target):
        return pltpu.make_async_remote_copy(
            src_ref=src,
            dst_ref=dst,
            send_sem=send,
            recv_sem=recv,
            device_id={"req": target},
            device_id_type=MESH,
        )

    def arrive(dst, recv):
        pltpu.make_async_copy(dst, dst, recv).wait()

    def each_hub(act):
        for j in range(hubs):

            @pl.when(hub_at(j) != me)
            def _():
                act(j)

    def to_hub_first(j):
        return remote(
            piece.at[j, 0 : rows + 1],
            hub_in.at[me, 0 : rows + 1],
            send_a.at[j],
            recv_a.at[me],
            hub_at(j),
        )

    def to_hub_back(j):
        return remote(
            r_out.at[j, 0:rows], hub_r.at[me, 0:rows], send_c.at[j], recv_c.at[me], hub_at(j)
        )

    def from_hub_first(i):
        return remote(
            hub_out.at[i, 0:rows], q_in.at[hub_rank, 0:rows], send_b.at[i], recv_b.at[hub_rank], i
        )

    final_at = pl.multiple_of(LEAD + room * hub_rank, 8)

    def from_hub_back(i):
        return remote(
            hub_f.at[i, 0:rows],
            final.at[pl.ds(final_at, rows)],
            send_d.at[i],
            recv_d.at[hub_rank],
            i,
        )

    far = jnp.where(me >= count // 2, 0, max(1, hubs // 2))
    for jj in range(hubs):
        far_j = lax.rem(far + jj, hubs)

        @pl.when(hub_at(far_j) != me)
        def _():
            to_hub_first(far_j).start()

    loads[2].wait()
    rows_of(q_v, a_v)
    for s in range(slots):
        a_v[s, 0:STEPS, :] = silu(a_v[s, 0:STEPS, :])
        a_v[s, STEPS:, :] = jnp.zeros((8 - STEPS, width), jnp.float32)
    loads[3].wait()
    loads[4].wait()
    rows_of(k_v, b_v)
    rows_of(v_v, c_v)
    for s in range(slots):
        b_v[s, 0:STEPS, :] = silu(b_v[s, 0:STEPS, :])
        c_v[s, 0:STEPS, :] = silu(c_v[s, 0:STEPS, :])
        b_v[s, STEPS:, :] = jnp.zeros((8 - STEPS, width), jnp.float32)
        c_v[s, STEPS:, :] = jnp.zeros((8 - STEPS, width), jnp.float32)

    for copy in state_loads:
        copy.wait()

    def halve(h, carry):
        for s in range(slots):
            for side in range(2):
                cols = slice(side * D_HEAD, (side + 1) * D_HEAD)
                high, low = split(s_v[s, 2 * h + side])
                s_pair[s, h, 0:D_HEAD, cols] = high.astype(jnp.bfloat16)
                s_pair[s, h, D_HEAD:, cols] = low.astype(jnp.bfloat16)
        return carry

    lax.fori_loop(0, heads // 2, halve, 0)

    planes = count // hubs
    near = planes // 2 - 1
    order = sorted(range(planes), key=lambda p: (-abs(p - near), -p))
    own_plane = me // hubs
    own_lane = lax.rem(me, hubs)

    def far_first(k):
        place = k // hubs
        plane = order[-1]
        for p in range(planes - 1):
            plane = jnp.where(place == p, order[p], plane)
        plane = jnp.where(own_plane == near, plane, planes - 1 - plane)
        lane = own_lane + lax.rem(k, hubs) + jnp.where(plane == own_plane, 1, 0)
        return plane * hubs + lax.rem(lane, hubs)

    def in_turn(k):
        return k + jnp.where(k >= me, 1, 0)

    hub_unroll = 3

    @pl.when(is_hub)
    def _():
        def gather(k, carry):
            arrive(hub_in.at[other(k), 0 : rows + 1], recv_a.at[other(k)])
            return carry

        lax.fori_loop(1, count, gather, 0)

        def choose(i):
            want = hub_in[i, rows : rows + 1, :]
            chosen = hub_in[0, 0:rows]
            for e in range(1, count):
                chosen = jnp.where(want == float(e), hub_in[e, 0:rows], chosen)
            return chosen

        def hand(k, carry):
            i = jnp.where(own_plane == near, count - 1 - (k + jnp.where(k >= count - 1 - me, 1, 0)), in_turn(k))
            hub_out[i, 0:rows] = choose(i)
            from_hub_first(i).start()
            return carry

        lax.fori_loop(0, count - 1, hand, 0, unroll=hub_unroll)
        q_in[hub_rank, 0:rows] = choose(me)

    piece_row = lax.broadcasted_iota(jnp.int32, (full, D_HEAD), 0)
    piece_head = jnp.zeros((full, D_HEAD), jnp.int32)
    for hh in range(1, per_hub):
        piece_head = jnp.where(piece_row >= GROUP * hh, hh, piece_head)
    piece_step = (piece_row - GROUP * piece_head).astype(jnp.float32)
    def fading(j, carry):
        slope = head_slope((piece_head + j * per_hub).astype(jnp.float32))
        fade[j, 0] = jnp.exp(-slope * (piece_step + (BEFORE + 1.0)))
        for s in range(BEFORE):
            fade[j, 1 + s] = jnp.exp(-slope * (piece_step + float(BEFORE - s)))
        return carry

    lax.fori_loop(0, hubs, fading, 0)
    for h in range(heads):
        j, hh = divmod(h, per_hub)
        cols = slice(h * D_HEAD, (h + 1) * D_HEAD)
        for s in range(BEFORE):
            early_k[s, j, GROUP * hh : GROUP * (hh + 1), :] = jnp.broadcast_to(
                b_v[moving, s : s + 1, cols], (GROUP, D_HEAD)
            )
            early_v[s, j, GROUP * hh : GROUP * (hh + 1), :] = jnp.broadcast_to(
                c_v[moving, s : s + 1, cols], (GROUP, D_HEAD)
            )

    step = lax.broadcasted_iota(jnp.int32, (8, D_HEAD), 0)
    step_f = step.astype(jnp.float32)

    def owns(*parts):
        def own(pair, carry):
            for s in range(slots):
                wide = pl.ds(pl.multiple_of(pair * 2 * D_HEAD, D_HEAD), 2 * D_HEAD)
                a_high, a_low = split(a_v[s, :, wide])
                left = jnp.concatenate(
                    [x[:, k * D_HEAD : (k + 1) * D_HEAD] for k in range(2) for x in (a_high, a_low)],
                    axis=0,
                )
                left = jnp.concatenate([left, left], axis=1).astype(jnp.bfloat16)
                pltpu.matmul_push_rhs(s_pair[s, pair], 0, s % 2)
                pltpu.matmul_acc_lhs(parts[s % 2], left, load_staged_rhs=0)
                product = pltpu.matmul_pop(parts[s % 2])
                for side in range(2):
                    h = 2 * pair + side
                    here = slice(side * D_HEAD, (side + 1) * D_HEAD)
                    cols = pl.ds(pl.multiple_of(h * D_HEAD, D_HEAD), D_HEAD)
                    slope = head_slope(jnp.full((8, D_HEAD), h, jnp.int32).astype(jnp.float32))
                    decay_state = jnp.exp(-slope * (step_f + 1.0))
                    a, b, c = a_v[s, :, cols], b_v[s, :, cols], c_v[s, :, cols]
                    both = product[16 * side : 16 * (side + 1), here]
                    base = decay_state * (both[:8] + both[8:])
                    within = jnp.zeros((8, D_HEAD), jnp.float32)
                    for back in range(STEPS):
                        b_back = pltpu.roll(b, back, 0) if back else b
                        c_back = pltpu.roll(c, back, 0) if back else c
                        mix = jnp.sum(a * b_back, axis=1, keepdims=True)
                        term = mix * c_back * jnp.exp(-slope * float(back))
                        late = (step >= BEFORE) & (step < STEPS)
                        if back < BEFORE:
                            keep = ((step < BEFORE) & (step >= back)) | (late & (step >= BEFORE + back))
                            within = within + jnp.where(keep, term, 0.0)
                        if back:
                            cross = late & (step >= back) & (step < BEFORE + back)
                            base = base + jnp.where(cross, term, 0.0)
                    base_v[s, :, cols] = base
                    w_v[s, :, cols] = within
            return carry

        lax.fori_loop(0, heads // 2, own, 0)

    pl.run_scoped(owns, *(pltpu.ACC(mxu_id=k)((32, 2 * D_HEAD), jnp.float32) for k in range(2)))

    pairs = per_hub // 2
    staged = min(4, pairs)

    def stage(j, begin):
        for k in range(min(staged, pairs - begin)):
            pltpu.matmul_push_rhs(s_pair[moving, j * pairs + begin + k], k // 2, k % 2)

    def replies(*sums):
        def answer(j):
            q = q_in[j, 0:full]
            high, low = split(q)
            left = jnp.concatenate([high, low], axis=0)
            left = jnp.concatenate([left, left], axis=1).astype(jnp.bfloat16)
            total = jnp.zeros((full, D_HEAD), jnp.float32)
            for begin in range(0, pairs, staged):
                if begin:
                    stage(j, begin)
                for k in range(min(staged, pairs - begin)):
                    pltpu.matmul_acc_lhs(sums[k], left, load_staged_rhs=k // 2)
                for k in range(min(staged, pairs - begin)):
                    both = pltpu.matmul_pop(sums[k])
                    both = both[:full] + both[full:]
                    for side in range(2):
                        total = jnp.where(
                            piece_head == 2 * (begin + k) + side,
                            both[:, side * D_HEAD : (side + 1) * D_HEAD],
                            total,
                        )
            total = total * fade[j, 0]
            for s in range(BEFORE):
                mix = jnp.sum(q * early_k[s, j, 0:full], axis=1, keepdims=True)
                total = total + mix * early_v[s, j, 0:full] * fade[j, 1 + s]
            r_out[j, 0:full] = total

        turn = jnp.where(me >= count // 2, 0, max(1, hubs // 2))

        def reply(jj, carry):
            j = jnp.where(me >= count // 2, jj, hubs - 1 - jj)
            stage(j, 0)

            @pl.when(hub_at(j) != me)
            def _():
                arrive(q_in.at[j, 0:rows], recv_b.at[j])

            answer(j)

            @pl.when(hub_at(j) != me)
            def _():
                to_hub_back(j).start()

            return carry

        lax.fori_loop(0, hubs, reply, 0)

    pl.run_scoped(
        replies,
        *(pltpu.ACC(mxu_id=k % 2)((2 * full, 2 * D_HEAD), jnp.float32) for k in range(staged)),
    )

    @pl.when(is_hub)
    def _():
        hub_r[me] = r_out[hub_rank]

    loads[5].wait()
    loads[6].wait()
    rows_of(g_v, scale_v)
    for s in range(slots):
        gate = scale_v[s, 0:STEPS, :]
        scale_v[s, 0:STEPS, :] = gain_v[...] / (1.0 + jnp.exp(-gate))
        scale_v[s, STEPS:, :] = jnp.zeros((8 - STEPS, width), jnp.float32)
    for s in range(slots):
        mixed = base_v[s] + w_v[s]
        energy = jnp.sum(mixed * mixed, axis=1, keepdims=True) * (1.0 / width)
        row = mixed * lax.rsqrt(energy + 1e-06) * scale_v[s]
        for t in range(STEPS):
            row_v[t, s : s + 1, :] = row[t : t + 1]
    for t in range(BEFORE):
        out_ref[t] = row_v[t].astype(out_ref.dtype)

    @pl.when(is_hub)
    def _():
        def gather(k, carry):
            arrive(hub_r.at[other(k), 0:rows], recv_c.at[other(k)])
            return carry

        lax.fori_loop(1, count, gather, 0)

        def choose(i):
            place = jnp.full((1, D_HEAD), i, jnp.int32).astype(jnp.float32)
            chosen = hub_r[0, 0:rows]
            for e in range(1, count):
                chosen = jnp.where(hub_in[e, rows : rows + 1, :] == place, hub_r[e, 0:rows], chosen)
            return chosen

        def back(k, carry):
            i = in_turn(k)
            hub_f[i, 0:rows] = choose(i)
            from_hub_back(i).start()
            return carry

        lax.fori_loop(0, count - 1, back, 0, unroll=hub_unroll)
        final[pl.ds(final_at, rows), :] = choose(me)

    each_hub(lambda j: to_hub_first(j).wait_send())
    each_hub(lambda j: to_hub_back(j).wait_send())

    each_hub(lambda j: arrive(final.at[pl.ds(LEAD + room * j, rows)], recv_d.at[j]))

    square = jnp.zeros((8, D_HEAD), jnp.float32)
    mixed = []
    for h in range(heads):
        top = LEAD + room * (h // per_hub) + GROUP * (h % per_hub) - BEFORE
        got = final[top : top + 8, :] + w_v[moving, :, h * D_HEAD : (h + 1) * D_HEAD]
        square = square + got * got
        mixed.append(got)
    energy = jnp.sum(square, axis=1, keepdims=True) * (1.0 / width)
    inverse = lax.rsqrt(energy + 1e-06)
    moved = lax.broadcasted_iota(jnp.int32, (slots, D_HEAD), 0) == moving
    for h in range(heads):
        cols = slice(h * D_HEAD, (h + 1) * D_HEAD)
        row = mixed[h] * inverse * scale_v[moving, :, cols]
        for t in range(BEFORE, STEPS):
            value = jnp.where(
                moved, jnp.broadcast_to(row[t : t + 1], (slots, D_HEAD)), row_v[t, :, cols]
            )
            out_ref[t, :, cols] = value.astype(out_ref.dtype)

    @pl.when(is_hub)
    def _():
        def drain(k, carry):
            from_hub_first(other(k)).wait_send()
            from_hub_back(other(k)).wait_send()
            return carry

        lax.fori_loop(1, count, drain, 0)


def on_device(queries, keys, values, gates, states, new_slot, norm_gain):
    queries, keys, values, gates = (x.transpose(1, 0, 2) for x in (queries, keys, values, gates))
    steps, slots, width = queries.shape
    heads = states.shape[1]
    count = lax.axis_size("req")
    hubs = max(1, min(count // 4, heads // 2))
    room = -(-(GROUP * (heads // hubs) + 1) // 8) * 8
    f32, bf16 = jnp.float32, jnp.bfloat16
    hbm = pl.BlockSpec(memory_space=pl.ANY)
    dma = pltpu.SemaphoreType.DMA
    slab = pltpu.VMEM((slots, 8, width), f32)
    return pl.pallas_call(
        functools.partial(kernel, count, hubs),
        out_shape=pltpu.VMEM(queries.shape, queries.dtype),
        in_specs=[hbm] * 7,
        out_specs=pl.BlockSpec(memory_space=pltpu.VMEM),
        scratch_shapes=[
            pltpu.SMEM(new_slot.shape, new_slot.dtype),
            pltpu.VMEM(queries.shape, bf16),
            pltpu.VMEM(queries.shape, bf16),
            pltpu.VMEM(queries.shape, bf16),
            pltpu.VMEM(queries.shape, bf16),
            pltpu.VMEM((1, width), f32),
            pltpu.VMEM(states.shape, f32),
            pltpu.VMEM((slots, heads // 2, 2 * D_HEAD, 2 * D_HEAD), bf16),
            slab,
            slab,
            slab,
            slab,
            slab,
            slab,
            pltpu.VMEM((steps, slots, width), f32),
            pltpu.VMEM((BEFORE, hubs, room, D_HEAD), f32),
            pltpu.VMEM((BEFORE, hubs, room, D_HEAD), f32),
            pltpu.VMEM((hubs, 1 + BEFORE, -(-GROUP * (heads // hubs) // 8) * 8, D_HEAD), f32),
            pltpu.VMEM((hubs, room, D_HEAD), f32),
            pltpu.VMEM((count, room, D_HEAD), f32),
            pltpu.VMEM((count, room, D_HEAD), f32),
            pltpu.VMEM((hubs, room, D_HEAD), f32),
            pltpu.VMEM((hubs, room, D_HEAD), f32),
            pltpu.VMEM((count, room, D_HEAD), f32),
            pltpu.VMEM((count, room, D_HEAD), f32),
            pltpu.VMEM((LEAD + room * hubs + 8, D_HEAD), f32),
            dma((7,)),
            dma((slots,)),
            dma((hubs,)),
            dma((count,)),
            dma((count,)),
            dma((hubs,)),
            dma((hubs,)),
            dma((count,)),
            dma((count,)),
            dma((hubs,)),
        ],
        compiler_params=pltpu.CompilerParams(collective_id=0, has_side_effects=True),
    )(new_slot, queries, keys, values, gates, norm_gain.reshape(1, width), states).transpose(
        1, 0, 2
    )


def solution(mesh):
    in_specs = (
        P(("groups", "req"), None, None),
        P(("groups", "req"), None, None),
        P(("groups", "req"), None, None),
        P(("groups", "req"), None, None),
        P(("groups", "req"), None, None, None),
        P(("groups", "req")),
        P(),
    )
    out_specs = P(("groups", "req"), None, None)
    return jax.shard_map(
        on_device, mesh=mesh, in_specs=in_specs, out_specs=out_specs, check_vma=False
    )
```

```python
import functools
import math

import jax
import jax.numpy as jnp
from jax import lax
from jax.experimental import pallas as pl
from jax.experimental.pallas import tpu as pltpu
from jax.sharding import PartitionSpec as P

D_HEAD = 128
BEFORE = 3
STEPS = 6
MODEL_HEADS = 64
GROUP = STEPS - BEFORE
LEAD = 8

MESH = pl.DeviceIdType.MESH


def silu(x):
    return x / (1.0 + jnp.exp(-x))


def split(x):
    high = x.astype(jnp.bfloat16).astype(jnp.float32)
    return high, x - high


def rows_of(src, dst):
    for t in range(STEPS):
        both = src[t].astype(jnp.float32)
        for s in range(both.shape[0]):
            dst[s, t : t + 1, :] = both[s : s + 1]


def head_slope(heads):
    return jnp.exp((heads + 1.0) * (-8.0 / MODEL_HEADS * math.log(2.0)))


def kernel(
    count,
    hubs,
    slot_hbm,
    q_hbm,
    k_hbm,
    v_hbm,
    g_hbm,
    gain_hbm,
    s_hbm,
    out_ref,
    slot_ref,
    q_v,
    k_v,
    v_v,
    g_v,
    gain_v,
    s_v,
    s_pair,
    a_v,
    b_v,
    c_v,
    w_v,
    base_v,
    scale_v,
    row_v,
    early_k,
    early_v,
    fade,
    piece,
    hub_in,
    hub_out,
    q_in,
    r_out,
    hub_r,
    hub_f,
    final,
    load_sem,
    state_sem,
    send_a,
    recv_a,
    send_b,
    recv_b,
    send_c,
    recv_c,
    send_d,
    recv_d,
):
    slots, heads = s_hbm.shape[0], s_hbm.shape[1]
    width = heads * D_HEAD
    per_hub = heads // hubs
    rows = GROUP * per_hub
    room = piece.shape[1]
    full = fade.shape[2]
    first = count // 2 - hubs
    me = lax.axis_index("req")
    is_hub = (me >= first) & (me < first + 2 * hubs) & (lax.rem(me, 2) == 1)
    hub_rank = jnp.clip(me - first, 0, 2 * hubs - 1) // 2

    def hub_at(j):
        return first + 2 * j + 1

    loads = [
        pltpu.make_async_copy(src, dst, load_sem.at[k])
        for k, (src, dst) in enumerate(
            (
                (slot_hbm, slot_ref),
                (q_hbm.at[BEFORE:], q_v.at[BEFORE:]),
                (q_hbm.at[:BEFORE], q_v.at[:BEFORE]),
                (k_hbm, k_v),
                (v_hbm, v_v),
                (g_hbm, g_v),
                (gain_hbm, gain_v),
            )
        )
    ]
    state_loads = [
        pltpu.make_async_copy(s_hbm.at[s], s_v.at[s], state_sem.at[s]) for s in range(slots)
    ]
    loads[0].start()
    loads[1].start()

    barrier = pltpu.get_barrier_semaphore()

    def other(k):
        return lax.rem(me + k, count)

    @pl.when(is_hub)
    def _():
        def greet(k, carry):
            pl.semaphore_signal(barrier, inc=1, device_id={"req": other(k)}, device_id_type=MESH)
            return carry

        lax.fori_loop(1, count, greet, 0, unroll=5 if (count - 1) % 5 == 0 else 1)

    for copy in loads[2:5] + state_loads + loads[5:]:
        copy.start()

    loads[0].wait()
    moving = jnp.int32(0)
    for s in range(slots):
        moving = jnp.where(slot_ref[s] != me * slots + s, jnp.int32(s), moving)
    wanted = slot_ref[moving] // slots
    wanted_row = jnp.full((1, D_HEAD), wanted, jnp.int32).astype(jnp.float32)

    loads[1].wait()
    span = per_hub * D_HEAD

    def pack(j, carry):
        cols = pl.ds(pl.multiple_of(j * span, D_HEAD), span)
        for t in range(GROUP):
            both = q_v[BEFORE + t, :, cols].astype(jnp.float32)
            raw = both[0:1]
            for s in range(1, slots):
                raw = jnp.where(moving == s, both[s : s + 1], raw)
            for hh in range(per_hub):
                row = GROUP * hh + t
                piece[j, row : row + 1, :] = raw[:, hh * D_HEAD : (hh + 1) * D_HEAD]
        piece[j, 0:rows, :] = silu(piece[j, 0:rows, :])
        piece[j, rows : rows + 1, :] = wanted_row
        return carry

    lax.fori_loop(0, hubs, pack, 0)

    @pl.when(is_hub)
    def _():
        hub_in[me] = piece[hub_rank]

    @pl.when(is_hub)
    def _():
        if hubs > 1:
            pl.semaphore_wait(barrier, hubs - 1)

    @pl.when(jnp.logical_not(is_hub))
    def _():
        pl.semaphore_wait(barrier, hubs)

    def remote(src, dst, send, recv, target):
        return pltpu.make_async_remote_copy(
            src_ref=src,
            dst_ref=dst,
            send_sem=send,
            recv_sem=recv,
            device_id={"req": target},
            device_id_type=MESH,
        )

    def arrive(dst, recv):
        pltpu.make_async_copy(dst, dst, recv).wait()

    def each_hub(act):
        for j in range(hubs):

            @pl.when(hub_at(j) != me)
            def _():
                act(j)

    def to_hub_first(j):
        return remote(
            piece.at[j, 0 : rows + 1],
            hub_in.at[me, 0 : rows + 1],
            send_a.at[j],
            recv_a.at[me],
            hub_at(j),
        )

    def to_hub_back(j):
        return remote(
            r_out.at[j, 0:rows], hub_r.at[me, 0:rows], send_c.at[j], recv_c.at[me], hub_at(j)
        )

    def from_hub_first(i):
        return remote(
            hub_out.at[i, 0:rows], q_in.at[hub_rank, 0:rows], send_b.at[i], recv_b.at[hub_rank], i
        )

    final_at = pl.multiple_of(LEAD + room * hub_rank, 8)

    def from_hub_back(i):
        return remote(
            hub_f.at[i, 0:rows],
            final.at[pl.ds(final_at, rows)],
            send_d.at[i],
            recv_d.at[hub_rank],
            i,
        )

    far = jnp.where(me >= count // 2, 0, max(1, hubs // 2))
    for jj in range(hubs):
        far_j = jnp.where(me >= count // 2, jj, hubs - 1 - jj)

        @pl.when(hub_at(far_j) != me)
        def _():
            to_hub_first(far_j).start()

    loads[2].wait()
    rows_of(q_v, a_v)
    for s in range(slots):
        a_v[s, 0:STEPS, :] = silu(a_v[s, 0:STEPS, :])
        a_v[s, STEPS:, :] = jnp.zeros((8 - STEPS, width), jnp.float32)
    loads[3].wait()
    loads[4].wait()
    rows_of(k_v, b_v)
    rows_of(v_v, c_v)
    for s in range(slots):
        b_v[s, 0:STEPS, :] = silu(b_v[s, 0:STEPS, :])
        c_v[s, 0:STEPS, :] = silu(c_v[s, 0:STEPS, :])
        b_v[s, STEPS:, :] = jnp.zeros((8 - STEPS, width), jnp.float32)
        c_v[s, STEPS:, :] = jnp.zeros((8 - STEPS, width), jnp.float32)

    for copy in state_loads:
        copy.wait()

    def halve(h, carry):
        for s in range(slots):
            for side in range(2):
                cols = slice(side * D_HEAD, (side + 1) * D_HEAD)
                high, low = split(s_v[s, 2 * h + side])
                s_pair[s, h, 0:D_HEAD, cols] = high.astype(jnp.bfloat16)
                s_pair[s, h, D_HEAD:, cols] = low.astype(jnp.bfloat16)
        return carry

    lax.fori_loop(0, heads // 2, halve, 0)

    planes = count // hubs
    near = planes // 2 - 1
    order = sorted(range(planes), key=lambda p: (-abs(p - near), -p))
    own_plane = me // hubs
    own_lane = lax.rem(me, hubs)

    def far_first(k):
        place = k // hubs
        plane = order[-1]
        for p in range(planes - 1):
            plane = jnp.where(place == p, order[p], plane)
        plane = jnp.where(own_plane == near, plane, planes - 1 - plane)
        lane = own_lane + lax.rem(k, hubs) + jnp.where(plane == own_plane, 1, 0)
        return plane * hubs + lax.rem(lane, hubs)

    def in_turn(k):
        return k + jnp.where(k >= me, 1, 0)

    hub_unroll = 5 if (count - 1) % 5 == 0 else 1

    @pl.when(is_hub)
    def _():
        def gather(k, carry):
            arrive(hub_in.at[other(k), 0 : rows + 1], recv_a.at[other(k)])
            return carry

        lax.fori_loop(1, count, gather, 0)

        def choose(i):
            want = hub_in[i, rows : rows + 1, :]
            chosen = hub_in[0, 0:rows]
            for e in range(1, count):
                chosen = jnp.where(want == float(e), hub_in[e, 0:rows], chosen)
            return chosen

        def hand(k, carry):
            i = jnp.where(own_plane == near, count - 1 - (k + jnp.where(k >= count - 1 - me, 1, 0)), in_turn(k))
            hub_out[i, 0:rows] = choose(i)
            from_hub_first(i).start()
            return carry

        lax.fori_loop(0, count - 1, hand, 0, unroll=hub_unroll)
        q_in[hub_rank, 0:rows] = choose(me)

    piece_row = lax.broadcasted_iota(jnp.int32, (full, D_HEAD), 0)
    piece_head = jnp.zeros((full, D_HEAD), jnp.int32)
    for hh in range(1, per_hub):
        piece_head = jnp.where(piece_row >= GROUP * hh, hh, piece_head)
    piece_step = (piece_row - GROUP * piece_head).astype(jnp.float32)
    def fading(j, carry):
        slope = head_slope((piece_head + j * per_hub).astype(jnp.float32))
        fade[j, 0] = jnp.exp(-slope * (piece_step + (BEFORE + 1.0)))
        for s in range(BEFORE):
            fade[j, 1 + s] = jnp.exp(-slope * (piece_step + float(BEFORE - s)))
        return carry

    lax.fori_loop(0, hubs, fading, 0)
    for h in range(heads):
        j, hh = divmod(h, per_hub)
        cols = slice(h * D_HEAD, (h + 1) * D_HEAD)
        for s in range(BEFORE):
            early_k[s, j, GROUP * hh : GROUP * (hh + 1), :] = jnp.broadcast_to(
                b_v[moving, s : s + 1, cols], (GROUP, D_HEAD)
            )
            early_v[s, j, GROUP * hh : GROUP * (hh + 1), :] = jnp.broadcast_to(
                c_v[moving, s : s + 1, cols], (GROUP, D_HEAD)
            )

    step = lax.broadcasted_iota(jnp.int32, (8, D_HEAD), 0)
    step_f = step.astype(jnp.float32)

    def owns(*parts):
        def own(pair, carry):
            for s in range(slots):
                wide = pl.ds(pl.multiple_of(pair * 2 * D_HEAD, D_HEAD), 2 * D_HEAD)
                a_high, a_low = split(a_v[s, :, wide])
                left = jnp.concatenate(
                    [x[:, k * D_HEAD : (k + 1) * D_HEAD] for k in range(2) for x in (a_high, a_low)],
                    axis=0,
                )
                left = jnp.concatenate([left, left], axis=1).astype(jnp.bfloat16)
                pltpu.matmul_push_rhs(s_pair[s, pair], 0, s % 2)
                pltpu.matmul_acc_lhs(parts[s % 2], left, load_staged_rhs=0)
                product = pltpu.matmul_pop(parts[s % 2])
                for side in range(2):
                    h = 2 * pair + side
                    here = slice(side * D_HEAD, (side + 1) * D_HEAD)
                    cols = pl.ds(pl.multiple_of(h * D_HEAD, D_HEAD), D_HEAD)
                    slope = head_slope(jnp.full((8, D_HEAD), h, jnp.int32).astype(jnp.float32))
                    decay_state = jnp.exp(-slope * (step_f + 1.0))
                    a, b, c = a_v[s, :, cols], b_v[s, :, cols], c_v[s, :, cols]
                    both = product[16 * side : 16 * (side + 1), here]
                    base = decay_state * (both[:8] + both[8:])
                    within = jnp.zeros((8, D_HEAD), jnp.float32)
                    for back in range(STEPS):
                        b_back = pltpu.roll(b, back, 0) if back else b
                        c_back = pltpu.roll(c, back, 0) if back else c
                        mix = jnp.sum(a * b_back, axis=1, keepdims=True)
                        term = mix * c_back * jnp.exp(-slope * float(back))
                        late = (step >= BEFORE) & (step < STEPS)
                        if back < BEFORE:
                            keep = ((step < BEFORE) & (step >= back)) | (late & (step >= BEFORE + back))
                            within = within + jnp.where(keep, term, 0.0)
                        if back:
                            cross = late & (step >= back) & (step < BEFORE + back)
                            base = base + jnp.where(cross, term, 0.0)
                    base_v[s, :, cols] = base
                    w_v[s, :, cols] = within
            return carry

        lax.fori_loop(0, heads // 2, own, 0)

    pl.run_scoped(owns, *(pltpu.ACC(mxu_id=k)((32, 2 * D_HEAD), jnp.float32) for k in range(2)))

    pairs = per_hub // 2
    staged = min(4, pairs)

    def stage(j, begin):
        for k in range(min(staged, pairs - begin)):
            pltpu.matmul_push_rhs(s_pair[moving, j * pairs + begin + k], k // 2, k % 2)

    def replies(*sums):
        def answer(j):
            q = q_in[j, 0:full]
            high, low = split(q)
            left = jnp.concatenate([high, low], axis=0)
            left = jnp.concatenate([left, left], axis=1).astype(jnp.bfloat16)
            total = jnp.zeros((full, D_HEAD), jnp.float32)
            for begin in range(0, pairs, staged):
                if begin:
                    stage(j, begin)
                for k in range(min(staged, pairs - begin)):
                    pltpu.matmul_acc_lhs(sums[k], left, load_staged_rhs=k // 2)
                for k in range(min(staged, pairs - begin)):
                    both = pltpu.matmul_pop(sums[k])
                    both = both[:full] + both[full:]
                    for side in range(2):
                        total = jnp.where(
                            piece_head == 2 * (begin + k) + side,
                            both[:, side * D_HEAD : (side + 1) * D_HEAD],
                            total,
                        )
            total = total * fade[j, 0]
            for s in range(BEFORE):
                mix = jnp.sum(q * early_k[s, j, 0:full], axis=1, keepdims=True)
                total = total + mix * early_v[s, j, 0:full] * fade[j, 1 + s]
            r_out[j, 0:full] = total

        turn = jnp.where(me >= count // 2, 0, max(1, hubs // 2))

        def reply(jj, carry):
            j = lax.rem(turn + jj, hubs)
            stage(j, 0)

            @pl.when(hub_at(j) != me)
            def _():
                arrive(q_in.at[j, 0:rows], recv_b.at[j])

            answer(j)

            @pl.when(hub_at(j) != me)
            def _():
                to_hub_back(j).start()

            return carry

        lax.fori_loop(0, hubs, reply, 0)

    pl.run_scoped(
        replies,
        *(pltpu.ACC(mxu_id=k % 2)((2 * full, 2 * D_HEAD), jnp.float32) for k in range(staged)),
    )

    @pl.when(is_hub)
    def _():
        hub_r[me] = r_out[hub_rank]

    loads[5].wait()
    loads[6].wait()
    rows_of(g_v, scale_v)
    for s in range(slots):
        gate = scale_v[s, 0:STEPS, :]
        scale_v[s, 0:STEPS, :] = gain_v[...] / (1.0 + jnp.exp(-gate))
        scale_v[s, STEPS:, :] = jnp.zeros((8 - STEPS, width), jnp.float32)
    for s in range(slots):
        mixed = base_v[s] + w_v[s]
        energy = jnp.sum(mixed * mixed, axis=1, keepdims=True) * (1.0 / width)
        row = mixed * lax.rsqrt(energy + 1e-06) * scale_v[s]
        for t in range(STEPS):
            row_v[t, s : s + 1, :] = row[t : t + 1]
    for t in range(BEFORE):
        out_ref[t] = row_v[t].astype(out_ref.dtype)

    @pl.when(is_hub)
    def _():
        def gather(k, carry):
            arrive(hub_r.at[other(k), 0:rows], recv_c.at[other(k)])
            return carry

        lax.fori_loop(1, count, gather, 0)

        def choose(i):
            place = jnp.full((1, D_HEAD), i, jnp.int32).astype(jnp.float32)
            chosen = hub_r[0, 0:rows]
            for e in range(1, count):
                chosen = jnp.where(hub_in[e, rows : rows + 1, :] == place, hub_r[e, 0:rows], chosen)
            return chosen

        def back(k, carry):
            i = in_turn(k)
            hub_f[i, 0:rows] = choose(i)
            from_hub_back(i).start()
            return carry

        lax.fori_loop(0, count - 1, back, 0, unroll=hub_unroll)
        final[pl.ds(final_at, rows), :] = choose(me)

    each_hub(lambda j: to_hub_first(j).wait_send())
    each_hub(lambda j: to_hub_back(j).wait_send())

    each_hub(lambda j: arrive(final.at[pl.ds(LEAD + room * j, rows)], recv_d.at[j]))

    square = jnp.zeros((8, D_HEAD), jnp.float32)
    mixed = []
    for h in range(heads):
        top = LEAD + room * (h // per_hub) + GROUP * (h % per_hub) - BEFORE
        got = final[top : top + 8, :] + w_v[moving, :, h * D_HEAD : (h + 1) * D_HEAD]
        square = square + got * got
        mixed.append(got)
    energy = jnp.sum(square, axis=1, keepdims=True) * (1.0 / width)
    inverse = lax.rsqrt(energy + 1e-06)
    moved = lax.broadcasted_iota(jnp.int32, (slots, D_HEAD), 0) == moving
    for h in range(heads):
        cols = slice(h * D_HEAD, (h + 1) * D_HEAD)
        row = mixed[h] * inverse * scale_v[moving, :, cols]
        for t in range(BEFORE, STEPS):
            value = jnp.where(
                moved, jnp.broadcast_to(row[t : t + 1], (slots, D_HEAD)), row_v[t, :, cols]
            )
            out_ref[t, :, cols] = value.astype(out_ref.dtype)

    @pl.when(is_hub)
    def _():
        def drain(k, carry):
            from_hub_first(other(k)).wait_send()
            from_hub_back(other(k)).wait_send()
            return carry

        lax.fori_loop(1, count, drain, 0)


def on_device(queries, keys, values, gates, states, new_slot, norm_gain):
    queries, keys, values, gates = (x.transpose(1, 0, 2) for x in (queries, keys, values, gates))
    steps, slots, width = queries.shape
    heads = states.shape[1]
    count = lax.axis_size("req")
    hubs = max(1, min(count // 4, heads // 2))
    room = -(-(GROUP * (heads // hubs) + 1) // 8) * 8
    f32, bf16 = jnp.float32, jnp.bfloat16
    hbm = pl.BlockSpec(memory_space=pl.ANY)
    dma = pltpu.SemaphoreType.DMA
    slab = pltpu.VMEM((slots, 8, width), f32)
    return pl.pallas_call(
        functools.partial(kernel, count, hubs),
        out_shape=pltpu.VMEM(queries.shape, queries.dtype),
        in_specs=[hbm] * 7,
        out_specs=pl.BlockSpec(memory_space=pltpu.VMEM),
        scratch_shapes=[
            pltpu.SMEM(new_slot.shape, new_slot.dtype),
            pltpu.VMEM(queries.shape, bf16),
            pltpu.VMEM(queries.shape, bf16),
            pltpu.VMEM(queries.shape, bf16),
            pltpu.VMEM(queries.shape, bf16),
            pltpu.VMEM((1, width), f32),
            pltpu.VMEM(states.shape, f32),
            pltpu.VMEM((slots, heads // 2, 2 * D_HEAD, 2 * D_HEAD), bf16),
            slab,
            slab,
            slab,
            slab,
            slab,
            slab,
            pltpu.VMEM((steps, slots, width), f32),
            pltpu.VMEM((BEFORE, hubs, room, D_HEAD), f32),
            pltpu.VMEM((BEFORE, hubs, room, D_HEAD), f32),
            pltpu.VMEM((hubs, 1 + BEFORE, -(-GROUP * (heads // hubs) // 8) * 8, D_HEAD), f32),
            pltpu.VMEM((hubs, room, D_HEAD), f32),
            pltpu.VMEM((count, room, D_HEAD), f32),
            pltpu.VMEM((count, room, D_HEAD), f32),
            pltpu.VMEM((hubs, room, D_HEAD), f32),
            pltpu.VMEM((hubs, room, D_HEAD), f32),
            pltpu.VMEM((count, room, D_HEAD), f32),
            pltpu.VMEM((count, room, D_HEAD), f32),
            pltpu.VMEM((LEAD + room * hubs + 8, D_HEAD), f32),
            dma((7,)),
            dma((slots,)),
            dma((hubs,)),
            dma((count,)),
            dma((count,)),
            dma((hubs,)),
            dma((hubs,)),
            dma((count,)),
            dma((count,)),
            dma((hubs,)),
        ],
        compiler_params=pltpu.CompilerParams(collective_id=0, has_side_effects=True),
    )(new_slot, queries, keys, values, gates, norm_gain.reshape(1, width), states).transpose(
        1, 0, 2
    )


def solution(mesh):
    in_specs = (
        P(("groups", "req"), None, None),
        P(("groups", "req"), None, None),
        P(("groups", "req"), None, None),
        P(("groups", "req"), None, None),
        P(("groups", "req"), None, None, None),
        P(("groups", "req")),
        P(),
    )
    out_specs = P(("groups", "req"), None, None)
    return jax.shard_map(
        on_device, mesh=mesh, in_specs=in_specs, out_specs=out_specs, check_vma=False
    )
```
